512 devices in a mesh: col: 8 (over y_lo, core), row: 8 (over z), tok: 8 (over y_hi, x).
Axes of the slice: x: 4, y: 8 (y_hi: 2, y_lo: 4; y = y_hi * 4 + y_lo), z: 8, core: 2. Of those that a mesh axis runs over, the one named last changes fastest.
Arguments:
- queries: bfloat16 [1024, 16384], P('tok', ('col', 'row')), may hold values from -512 to 512
- key_rows: bfloat16 [1024, 16384], P('tok', ('col', 'row')), may hold values from -12 to 12
- values: bfloat16 [1024, 16384], P('tok', ('col', 'row')), may hold values from -6 to 6
- code_first: int32 [16384, 2048], P(('row', 'tok'), 'col'), may hold values from 0 to 255
- code_second: int32 [16384, 2048], P(('row', 'tok'), 'col'), may hold values from 0 to 255
- book_first: bfloat16 [256, 8], replicated, may hold values from -0.59765625 to 0.59765625
- book_second: bfloat16 [256, 8], replicated, may hold values from -0.59765625 to 0.59765625
- scales: float32 [16384], P(('row', 'tok')), may hold values from 0.015 to 0.15
- target: bfloat16 [1024, 16384], P(None, ('row', 'tok')), may hold values from -2 to 2
Outputs:
- misfit: bfloat16 [1024, 16384], P(None, ('row', 'tok'))
- grad_scales: float32 [16384], P(('row', 'tok'))
- grad_books: float32 [2, 256, 8], replicated
The draws below stay inside these ranges and needn't reach their ends.
All inputs are finite; a program needn't handle non-finite values.
Results may differ from the reference program's by a relative error of at most 0.0053.
Values may be sent and summed in bfloat16 or wider, within the bound.
No kernel may reach another device: no remote copies, remote signals or barrier semaphores. Data moves between devices by JAX's collectives and lax.ppermute only.
A program may use at most 64 MiB of HBM per device.

```python
import math
import jax
import jax.numpy as jnp
from jax import lax

HEADS = 128
HEAD_DIM = 128
ENTRIES = 256
GROUP = 8
D = 16384
TOKENS = 1024


def draw_pair(key):
    base = jax.random.fold_in(key, 41)
    key_query, key_key = jax.random.split(base, 2)
    key_field = jax.random.normal(key_key, (TOKENS, HEADS, HEAD_DIM), jnp.float32)
    query_field = jax.random.normal(key_query, (TOKENS, HEADS, HEAD_DIM), jnp.float32)
    key_field = jnp.clip(key_field, -6.0, 6.0)
    query_field = jnp.clip(query_field, -6.0, 6.0)
    return (query_field.reshape(TOKENS, HEADS * HEAD_DIM), key_field.reshape(TOKENS, HEADS * HEAD_DIM))


def draw_queries(key, part):
    return draw_pair(key)[0].astype(jnp.bfloat16)


def draw_key_rows(key, part):
    return draw_pair(key)[1].astype(jnp.bfloat16)


def with_ends(drawn, own_key, low, largest):
    spot = [jax.random.randint(jax.random.fold_in(own_key, axis), (), 0, length) for axis, length in enumerate(drawn.shape)]
    main_axis = drawn.shape.index(max(drawn.shape))
    beside = spot[:main_axis] + [(spot[main_axis] + 1) % drawn.shape[main_axis]] + spot[main_axis + 1:]
    return drawn.at[tuple(spot)].set(low).at[tuple(beside)].set(largest)


def shard_levels(stream_key, shape, cuts, least, top_value):
    def one(axis_at, shards_of):
        heights = jax.random.uniform(jax.random.fold_in(jax.random.fold_in(stream_key, 6), axis_at), (shards_of,), jnp.float32, least / len(cuts), top_value / len(cuts))
        return jnp.repeat(jnp.exp(heights), shape[axis_at] // shards_of).reshape((-1,) + (1,) * (len(shape) - axis_at - 1))

    factor_of = one(*cuts[0])
    for cut in cuts[1:]:
        factor_of = factor_of * one(*cut)
    return factor_of


def noise(stream_key, extent, deviation, reach, cuts=(), kind=jnp.bfloat16):
    level = shard_levels(stream_key, extent, cuts, -0.22, 0.18) if cuts else 1.0
    entries = jax.random.normal(stream_key, extent, jnp.float32) * deviation * level
    return jnp.minimum(jnp.maximum(entries, -reach), reach).astype(kind)


def setup_inputs(seed: int = 0) -> dict:
    seeds = jax.random.split(jax.random.key(seed), 10)
    return {
        "queries": draw_queries(jax.random.fold_in(seeds[9], 71), 0),
        "key_rows": draw_key_rows(jax.random.fold_in(seeds[9], 71), 0),
        "values": noise(seeds[2], (TOKENS, D), 1.0, 6.0, ((0, 8), (1, 64))),
        "code_first": with_ends(jax.random.randint(seeds[3], (D, D // GROUP), 0, ENTRIES), jax.random.fold_in(seeds[3], 1), 0, ENTRIES - 1).astype(jnp.int32),
        "code_second": with_ends(jax.random.randint(seeds[4], (D, D // GROUP), 0, ENTRIES), jax.random.fold_in(seeds[4], 1), 0, ENTRIES - 1).astype(jnp.int32),
        "book_first": noise(seeds[5], (ENTRIES, GROUP), 0.1, 0.59765625),
        "book_second": noise(seeds[6], (ENTRIES, GROUP), 0.1, 0.59765625),
        "scales": jnp.clip(jnp.exp(math.log(0.15) - 2.3025852 * jax.random.uniform(seeds[7], (D,), jnp.float32) ** shard_levels(seeds[7], (D,), ((0, 64),), -0.2, 0.2)), 0.015, 0.15),
        "target": noise(seeds[8], (TOKENS, D), 0.3, 2.0, ((1, 64),)),
    }


def attend_head(operands):
    query_head, key_head, value_head = operands
    scores = jnp.dot(query_head, key_head.T, preferred_element_type=jnp.float32) / math.sqrt(HEAD_DIM)
    places = jnp.arange(scores.shape[0], dtype=jnp.int32)
    allowed = places[None, :] <= places[:, None]
    row_max = lax.optimization_barrier(jnp.max(jnp.where(allowed, scores, -jnp.inf), axis=1, keepdims=True))
    exponent = jnp.where(allowed, jnp.exp(scores - row_max), 0.0)
    row_sum = lax.optimization_barrier(jnp.sum(exponent, axis=1, keepdims=True))
    probs = exponent.astype(jnp.bfloat16)
    return jnp.dot(probs, value_head, preferred_element_type=jnp.float32) / row_sum

def split_heads(matrix):
    return matrix.reshape(TOKENS, HEADS, HEAD_DIM).transpose(1, 0, 2)

def reference(queries, key_rows, values, code_first, code_second, book_first, book_second, scales, target):
    heads_out = lax.map(attend_head, (split_heads(queries), split_heads(key_rows), split_heads(values)))
    attended = heads_out.transpose(1, 0, 2).reshape(TOKENS, D).astype(jnp.bfloat16)
    block_rows = math.gcd(D, 1024)
    count_blocks = D // block_rows
    first_book = book_first.astype(jnp.float32)
    second_book = book_second.astype(jnp.float32)

    def project(books_sum, operands):
        first_codes, second_codes, block_scales, block_target = operands
        unscaled = (jnp.take(first_book, first_codes, axis=0) + jnp.take(second_book, second_codes, axis=0)).reshape(block_rows, D)
        weight = (block_scales[:, None] * unscaled).astype(jnp.bfloat16)
        output = lax.dot_general(attended, weight, (((1,), (1,)), ((), ())), preferred_element_type=jnp.float32)
        misfit = (output - block_target.astype(jnp.float32)).astype(jnp.bfloat16)
        weight_grad = lax.dot_general(misfit, attended, (((0,), (0,)), ((), ())), preferred_element_type=jnp.float32) / TOKENS
        scale_grad = lax.optimization_barrier(jnp.sum(weight_grad * unscaled, axis=1))
        scaled = (block_scales[:, None] * weight_grad).reshape(-1, GROUP)
        book_terms = jnp.stack([jax.ops.segment_sum(scaled, first_codes.reshape(-1), ENTRIES), jax.ops.segment_sum(scaled, second_codes.reshape(-1), ENTRIES)])
        return (books_sum + book_terms, (misfit, scale_grad))
    targets_split = target.reshape(TOKENS, count_blocks, block_rows).transpose(1, 0, 2)
    initial = jnp.zeros((2, ENTRIES, GROUP), jnp.float32)
    grad_books, (misfit_blocks, scale_blocks) = lax.scan(project, initial, (code_first.reshape(count_blocks, block_rows, D // GROUP), code_second.reshape(count_blocks, block_rows, D // GROUP), scales.reshape(count_blocks, block_rows), targets_split))
    misfit = misfit_blocks.transpose(1, 0, 2).reshape(TOKENS, D)
    return (misfit, scale_blocks.reshape(D), grad_books)
```

```python
import math

import jax
import jax.numpy as jnp
from jax import lax
from jax.experimental import pallas as pl
from jax.experimental.pallas import tpu as pltpu
from jax.sharding import Mesh
from jax.sharding import PartitionSpec as P

HEAD_DIM = 128
ENTRIES = 256
GROUP = 8
LOW = 8
HIGH = ENTRIES // LOW
TOK = ("tok_0", "tok_1")
ROW_TOK = ("row", "tok_0", "tok_1")
COL = ("col_0", "col_1")
COL_ROW = ("col_0", "col_1", "row")
f32, bf16 = jnp.float32, jnp.bfloat16


def exchange(pieces, axis):
    return lax.all_to_all(pieces, axis, 0, 0, tiled=True)


def copies(array, axis):
    return exchange(jnp.broadcast_to(array[None], (lax.axis_size(axis), *array.shape)), axis)


def swap(array, axis):
    return lax.ppermute(array, axis, [(0, 1), (1, 0)])


def in_order(mine, theirs, place):
    first = place == 0
    return jnp.where(first, mine, theirs), jnp.where(first, theirs, mine)


def dequant_kernel(codes_ref, table_ref, scale_ref, out_ref):
    groups, rows = codes_ref.shape
    tables = [table_ref[i] for i in range(4)]
    scale = jnp.broadcast_to(scale_ref[...], (GROUP, rows))

    def group_rows(g):
        both = jnp.broadcast_to(codes_ref[pl.ds(g, 1), :], (GROUP, rows))
        parts = []
        for at in range(0, rows, 128):
            packed = both[:, at : at + 128]
            total = None
            for book in range(2):
                code = (packed & 255) if book == 0 else (packed >> 8)
                place = code & 127
                near = jnp.take_along_axis(tables[2 * book], place, axis=1)
                far = jnp.take_along_axis(tables[2 * book + 1], place, axis=1)
                entry = jnp.where(code >= 128, far, near)
                total = entry if total is None else total + entry
            parts.append(total * scale[:, at : at + 128])
        return jnp.concatenate(parts, axis=1)

    def step(i, carry):
        for k in range(4):
            pair = [group_rows(i * 8 + 2 * k + n) for n in range(2)]
            start = pl.multiple_of(i * 64 + 16 * k, 16)
            out_ref[pl.ds(start, 16), :] = jnp.concatenate(pair, axis=0).astype(bf16)
        return carry

    lax.fori_loop(0, groups // 8, step, 0)


def dequantize(codes, table, scales):
    blocks, groups, rows = codes.shape
    return pl.pallas_call(
        dequant_kernel,
        grid=(blocks,),
        in_specs=[
            pl.BlockSpec((None, groups, rows), lambda i: (i, 0, 0)),
            pl.BlockSpec((4, GROUP, 128), lambda i: (0, 0, 0)),
            pl.BlockSpec((None, 1, rows), lambda i: (i, 0, 0)),
        ],
        out_specs=pl.BlockSpec((None, groups * GROUP, rows), lambda i: (i, 0, 0)),
        out_shape=jax.ShapeDtypeStruct((blocks, groups * GROUP, rows), bf16),
        name="dequant",
    )(codes, table, scales)


def project_kernel(core_ref, att_ref, weight_ref, keep_ref, send_ref):
    steps, tokens, width = att_ref.shape
    half = tokens // 2
    for out_ref, who in ((send_ref, 1 - core_ref[0]), (keep_ref, core_ref[0])):
        start = pl.multiple_of(who * half, half)
        total = None
        for z in range(steps):
            part = jnp.dot(
                att_ref[z, pl.ds(start, half), :],
                weight_ref[z * width : (z + 1) * width, :],
                preferred_element_type=f32,
            )
            total = part if total is None else total + part
        out_ref[...] = total


def project(core, attended, weight):
    steps, tokens, width = attended.shape
    blocks, depth, rows = weight.shape
    out = jax.ShapeDtypeStruct((tokens // 2, blocks * rows), f32)
    out_spec = pl.BlockSpec((tokens // 2, rows), lambda i, core: (0, i))
    return pl.pallas_call(
        project_kernel,
        grid_spec=pltpu.PrefetchScalarGridSpec(
            num_scalar_prefetch=1,
            grid=(blocks,),
            in_specs=[
                pl.BlockSpec((steps, tokens, width), lambda i, core: (0, 0, 0)),
                pl.BlockSpec((None, depth, rows), lambda i, core: (i, 0, 0)),
            ],
            out_specs=[out_spec, out_spec],
        ),
        out_shape=[out, out],
        name="project",
    )(core, attended, weight)


def grads_kernel(scaling, att_ref, misfit_ref, weight_ref, codes_ref, scale_ref, gs_ref, bins_ref):
    block, step = pl.program_id(0), pl.program_id(1)
    width, rows = weight_ref.shape
    groups = width // GROUP
    weight_grad = (
        lax.dot_general(
            att_ref[...], misfit_ref[...], (((0,), (0,)), ((), ())), preferred_element_type=f32
        )
        * scaling
    )

    @pl.when(step == 0)
    def _():
        gs_ref[...] = jnp.zeros_like(gs_ref)

    @pl.when((block == 0) & (step == 0))
    def _():
        bins_ref[...] = jnp.zeros_like(bins_ref)

    weighted = weight_grad * weight_ref[...].astype(f32)
    gs_ref[...] += jnp.sum(weighted.reshape(groups, GROUP, rows), axis=0)
    scaled = weight_grad * scale_ref[...]
    at = lax.broadcasted_iota(jnp.int32, (16, rows), 0)
    low_rows = [(2 * d + (at >= 8).astype(jnp.int32)).astype(f32).astype(bf16) for d in range(LOW // 2)]
    high_rows = [(16 * d + at).astype(f32).astype(bf16) for d in range(HIGH // 16)]
    zero, one = jnp.zeros((16, rows), bf16), jnp.ones((16, rows), bf16)
    for book in range(2):
        total = None
        for start in range(0, groups, 8):
            highs, lows = [], []
            for g in range(start, start + 8):
                entry = scaled[GROUP * g : GROUP * (g + 1), :]
                twice = jnp.concatenate([entry, entry], axis=0).astype(bf16)
                packed = codes_ref[g : g + 1, :]
                code = (packed & 255) if book == 0 else (packed >> 8)
                low = jnp.broadcast_to((code & (LOW - 1)).astype(f32), (16, rows)).astype(bf16)
                high = jnp.broadcast_to((code >> 3).astype(f32), (16, rows)).astype(bf16)
                lows.append(jnp.concatenate([jnp.where(low == r, twice, zero) for r in low_rows], axis=0))
                highs.append(jnp.concatenate([jnp.where(high == r, one, zero) for r in high_rows], axis=0))
            part = lax.dot_general(
                jnp.concatenate(highs, axis=1),
                jnp.concatenate(lows, axis=1),
                (((1,), (1,)), ((), ())),
                preferred_element_type=f32,
            )
            total = part if total is None else total + part
        bins_ref[book] += total


def gradients(attended, misfit, weight, codes, scales, scaling):
    steps, tokens, width = attended.shape
    blocks, depth, rows = weight.shape
    return pl.pallas_call(
        lambda *refs: grads_kernel(scaling, *refs),
        grid=(blocks, steps),
        in_specs=[
            pl.BlockSpec((None, tokens, width), lambda i, z: (z, 0, 0)),
            pl.BlockSpec((tokens, rows), lambda i, z: (0, i)),
            pl.BlockSpec((None, width, rows), lambda i, z: (i, z, 0)),
            pl.BlockSpec((None, width // GROUP, rows), lambda i, z: (i, z, 0)),
            pl.BlockSpec((None, 1, rows), lambda i, z: (i, 0, 0)),
        ],
        out_specs=[
            pl.BlockSpec((None, GROUP, rows), lambda i, z: (i, 0, 0)),
            pl.BlockSpec((2, HIGH, LOW * GROUP), lambda i, z: (0, 0, 0)),
        ],
        out_shape=[
            jax.ShapeDtypeStruct((blocks, GROUP, rows), f32),
            jax.ShapeDtypeStruct((2, HIGH, LOW * GROUP), f32),
        ],
        name="grads",
    )(attended, misfit, weight, codes, scales)


def attend(queries, keys, values, places):
    scores = jnp.einsum("qd,kd->qk", queries, keys, preferred_element_type=f32) / math.sqrt(HEAD_DIM)
    allowed = lax.iota(jnp.int32, keys.shape[0])[None, :] <= places[:, None]
    row_max = jnp.max(jnp.where(allowed, scores, -1e30), axis=-1, keepdims=True)
    exponent = jnp.where(allowed, jnp.exp(scores - row_max), 0.0)
    row_sum = jnp.sum(exponent, axis=-1, keepdims=True)
    weighted = jnp.einsum("qk,kd->qd", exponent.astype(bf16), values, preferred_element_type=f32)
    return (weighted / row_sum).astype(bf16)


def local(
    queries, key_rows, values, code_first, code_second, book_first, book_second, scales, target
):
    tok_rows, width = queries.shape
    high, across = lax.axis_index("tok_0"), lax.axis_index("tok_1")
    count_across = lax.axis_size("tok_1")
    lane, core = lax.axis_index("col_0"), lax.axis_index("col_1")
    count_lane = lax.axis_size("col_0")
    rows = code_first.shape[0]
    tokens = lax.axis_size(TOK) * tok_rows

    def of_head(array, head):
        return lax.dynamic_slice_in_dim(array, head * HEAD_DIM, HEAD_DIM, 1)

    their_queries = swap(of_head(queries, 1 - high), "tok_0")
    pairs = jnp.stack(
        [jnp.concatenate([of_head(key_rows, h), of_head(values, h)], axis=1) for h in range(2)]
    )
    pairs = jnp.broadcast_to(pairs[:, None], (2, count_across, tok_rows, 2 * HEAD_DIM))
    pairs = exchange(pairs.reshape(-1, tok_rows, 2 * HEAD_DIM), TOK).reshape(tokens, 2 * HEAD_DIM)
    own_queries = jnp.concatenate(in_order(of_head(queries, high), their_queries, high), axis=0)
    place = across * tok_rows + lax.iota(jnp.int32, tok_rows)
    places = jnp.concatenate([place, place + count_across * tok_rows])
    head_out = attend(own_queries, pairs[:, :HEAD_DIM], pairs[:, HEAD_DIM:], places)
    head_out = jnp.concatenate(in_order(head_out, swap(head_out, "tok_0"), high), axis=1)
    attended = copies(head_out, "row")

    codes = copies((code_first + ENTRIES * code_second).T, "tok_1")
    half_tokens = tok_rows
    share = half_tokens // count_lane
    own_target = target.reshape(2, count_across, count_lane, share, rows)
    own_target = lax.dynamic_index_in_dim(own_target, core, 0, keepdims=False)
    own_target = lax.dynamic_index_in_dim(own_target, lane, 1, keepdims=False)
    row_scales = jnp.broadcast_to(scales[None, None], (count_across, 8, rows))
    side = exchange(jnp.concatenate([own_target.astype(f32), row_scales], axis=1), "tok_1")
    own_target, row_scales = side[:, :share], side[:, share : share + 1]
    books = jnp.stack([book_first, book_second]).astype(f32).transpose(0, 2, 1)
    table = books.reshape(2, GROUP, 2, 128).transpose(0, 2, 1, 3).reshape(4, GROUP, 128)
    weight = dequantize(codes, table, row_scales)

    keep, send = project(core.astype(jnp.int32)[None], attended, weight)
    half_sum = (keep + swap(send, "col_1")).astype(bf16)
    parts = exchange(half_sum.reshape(count_lane, share, -1), "col_0")
    output = jnp.sum(parts.astype(f32), axis=0)
    wanted = own_target.transpose(1, 0, 2).reshape(share, -1)
    misfit_share = (output - wanted).astype(bf16)
    misfit_half = copies(misfit_share, "col_0").reshape(half_tokens, -1)
    misfit = jnp.concatenate(in_order(misfit_half, swap(misfit_half, "col_1"), core), axis=0)

    by_rows = misfit.reshape(2 * tok_rows, count_across, rows).transpose(1, 0, 2)
    by_tokens = exchange(by_rows, "tok_1").reshape(count_across, 2, tok_rows, rows)
    misfit_out = by_tokens.transpose(1, 0, 2, 3).reshape(tokens, rows)

    scale_part, bins = gradients(attended, misfit, weight, codes, row_scales, 1.0 / tokens)
    scale_part = jnp.sum(scale_part, axis=1) / row_scales[:, 0]
    scale_part = scale_part.reshape(count_across, -1, 128)
    extra = scale_part.shape[1]
    bins = jnp.broadcast_to(bins.reshape(1, -1, 128), (count_across, 2 * ENTRIES * GROUP // 128, 128))
    sums = jnp.sum(exchange(jnp.concatenate([scale_part, bins], axis=1), "tok_1"), axis=0)
    sums = jnp.sum(copies(sums, COL), axis=0)
    grad_scales = sums[:extra].reshape(rows)
    bins = jnp.sum(copies(sums[extra:], ("row", "tok_0")), axis=0)
    return misfit_out, grad_scales, bins.reshape(2, ENTRIES, GROUP)


def solution(mesh):
    split = Mesh(
        mesh.devices.reshape(4, 2, mesh.shape["row"], 2, 4),
        ("col_0", "col_1", "row", "tok_0", "tok_1"),
    )
    return jax.shard_map(
        local,
        mesh=split,
        in_specs=(
            P(TOK, COL_ROW),
            P(TOK, COL_ROW),
            P(TOK, COL_ROW),
            P(ROW_TOK, COL),
            P(ROW_TOK, COL),
            P(),
            P(),
            P(ROW_TOK),
            P(None, ROW_TOK),
        ),
        out_specs=(P(None, ROW_TOK), P(ROW_TOK), P()),
        check_vma=False,
    )
```

```python
import math

import jax
import jax.numpy as jnp
from jax import lax
from jax.experimental import pallas as pl
from jax.experimental.pallas import tpu as pltpu
from jax.sharding import Mesh
from jax.sharding import PartitionSpec as P


HEAD_DIM = 128
ENTRIES = 256
GROUP = 8
LOW = 8
HIGH = ENTRIES // LOW
TOK = ("tok_0", "tok_1")
ROW_TOK = ("row", "tok_0", "tok_1")
COL = ("col_0", "col_1")
COL_ROW = ("col_0", "col_1", "row")
f32, bf16 = jnp.float32, jnp.bfloat16


def exchange(pieces, axis):
    return lax.all_to_all(pieces, axis, 0, 0, tiled=True)


def copies(array, axis):
    pieces = jnp.broadcast_to(array[None], (lax.axis_size(axis), *array.shape))
    return exchange(pieces, axis)


def swap(array, axis):
    return lax.ppermute(array, axis, [(0, 1), (1, 0)])


def in_order(mine, theirs, place):
    first = place == 0
    return jnp.where(first, mine, theirs), jnp.where(first, theirs, mine)


def dequant_kernel(codes_ref, table_ref, scale_ref, out_ref):
    groups, rows = codes_ref.shape
    tables = [table_ref[i] for i in range(4)]
    scale = jnp.broadcast_to(scale_ref[...], (GROUP, rows))

    def group_rows(g):
        both = jnp.broadcast_to(codes_ref[pl.ds(g, 1), :], (GROUP, rows)).astype(jnp.int32)
        parts = []
        for at in range(0, rows, 128):
            packed = both[:, at : at + 128]
            total = None
            for book in range(2):
                code = (packed & 255) if book == 0 else (packed >> 8)
                place = code & 127
                near = jnp.take_along_axis(tables[2 * book], place, axis=1)
                far = jnp.take_along_axis(tables[2 * book + 1], place, axis=1)
                entry = jnp.where(code >= 128, far, near)
                total = entry if total is None else total + entry
            parts.append(total * scale[:, at : at + 128])
        return jnp.concatenate(parts, axis=1)

    def step(i, carry):
        for k in range(4):
            pair = [group_rows(i * 8 + 2 * k + n) for n in range(2)]
            start = pl.multiple_of(i * 64 + 16 * k, 16)
            out_ref[pl.ds(start, 16), :] = jnp.concatenate(pair, axis=0).astype(bf16)
        return carry

    lax.fori_loop(0, groups // 8, step, 0)


def dequantize(codes, table, scales):
    blocks, groups, rows = codes.shape
    return pl.pallas_call(
        dequant_kernel,
        grid=(blocks,),
        in_specs=[
            pl.BlockSpec((None, groups, rows), lambda i: (i, 0, 0)),
            pl.BlockSpec((4, GROUP, 128), lambda i: (0, 0, 0)),
            pl.BlockSpec((None, 1, rows), lambda i: (i, 0, 0)),
        ],
        out_specs=pl.BlockSpec((None, groups * GROUP, rows), lambda i: (i, 0, 0)),
        out_shape=jax.ShapeDtypeStruct((blocks, groups * GROUP, rows), bf16),
        cost_estimate=pl.CostEstimate(
            flops=blocks * 8_000_000_000, transcendentals=0, bytes_accessed=blocks * 1_500_000
        ),
        name="dequant",
    )(codes, table, scales)


def project_kernel(place_ref, att_ref, own_ref, others_ref, keep_ref, send_ref):
    steps, tokens, width = att_ref.shape
    half = tokens // 2

    def one(weight_ref):
        for out_ref, who in ((send_ref, 1 - place_ref[1]), (keep_ref, place_ref[1])):
            start = pl.multiple_of(who * half, half)
            total = None
            for z in range(steps):
                part = jnp.dot(
                    att_ref[z, pl.ds(start, half), :],
                    weight_ref[z * width : (z + 1) * width, :],
                    preferred_element_type=f32,
                )
                total = part if total is None else total + part
            out_ref[...] = total

    pl.when(pl.program_id(0) == 0)(lambda: one(own_ref))
    pl.when(pl.program_id(0) > 0)(lambda: one(others_ref))


def project(place, attended, own, others):
    steps, tokens, width = attended.shape
    blocks, depth, rows = others.shape
    blocks += 1
    out = jax.ShapeDtypeStruct((tokens // 2, blocks * rows), f32)
    out_spec = pl.BlockSpec((tokens // 2, rows), lambda i, place: (0, (place[0] + i) % blocks))
    return pl.pallas_call(
        project_kernel,
        grid_spec=pltpu.PrefetchScalarGridSpec(
            num_scalar_prefetch=1,
            grid=(blocks,),
            in_specs=[
                pl.BlockSpec((steps, tokens, width), lambda i, place: (0, 0, 0)),
                pl.BlockSpec((None, depth, rows), lambda i, place: (0, 0, 0)),
                pl.BlockSpec((None, depth, rows), lambda i, place: (jnp.maximum(i - 1, 0), 0, 0)),
            ],
            out_specs=[out_spec, out_spec],
        ),
        out_shape=[out, out],
        name="project",
    )(place, attended, own, others)


def bins_kernel(scaling, att_ref, misfit_ref, codes_ref, scale_ref, bins_ref, grad_ref, digit_ref):
    groups, rows = codes_ref.shape
    steps, _, width = att_ref.shape
    scale = scale_ref[...] * scaling
    misfit = misfit_ref[...]
    for z in range(steps):
        weight_grad = lax.dot_general(
            att_ref[z], misfit, (((0,), (0,)), ((), ())), preferred_element_type=f32
        )
        grad_ref[z * width : (z + 1) * width, :] = weight_grad * scale
    packed = codes_ref[...].astype(jnp.int32)
    for book in range(2):
        code = (packed & 255) if book == 0 else (packed >> 8)
        digit_ref[2 * book] = (code & (LOW - 1)).astype(f32)
        digit_ref[2 * book + 1] = (code >> 3).astype(f32)
    at = lax.broadcasted_iota(jnp.int32, (16, rows), 0)
    low_rows = [(2 * d + (at >= 8).astype(jnp.int32)).astype(f32).astype(bf16) for d in range(LOW // 2)]
    high_rows = [(16 * d + at).astype(f32).astype(bf16) for d in range(HIGH // 16)]
    zero, one = jnp.zeros((16, rows), bf16), jnp.ones((16, rows), bf16)
    chunk = 8

    def digit(which, g):
        return jnp.broadcast_to(digit_ref[which, pl.ds(g, 1), :], (16, rows)).astype(bf16)

    def step(i, totals):
        twice = []
        for k in range(chunk):
            entry = grad_ref[pl.ds(pl.multiple_of((i * chunk + k) * GROUP, GROUP), GROUP), :]
            twice.append(jnp.concatenate([entry, entry], axis=0).astype(bf16))
        done = []
        for book in range(2):
            highs, lows = [], []
            for k in range(chunk):
                low, high = digit(2 * book, i * chunk + k), digit(2 * book + 1, i * chunk + k)
                lows.append(
                    jnp.concatenate([jnp.where(low == r, twice[k], zero) for r in low_rows], axis=0)
                )
                highs.append(
                    jnp.concatenate([jnp.where(high == r, one, zero) for r in high_rows], axis=0)
                )
            part = lax.dot_general(
                jnp.concatenate(highs, axis=1),
                jnp.concatenate(lows, axis=1),
                (((1,), (1,)), ((), ())),
                preferred_element_type=f32,
            )
            done.append(totals[book] + part)
        return tuple(done)

    empty = jnp.zeros((HIGH, LOW * GROUP), f32)
    totals = lax.fori_loop(0, groups // chunk, step, (empty, empty), unroll=2)

    @pl.when(pl.program_id(0) == 0)
    def _():
        bins_ref[...] = jnp.zeros_like(bins_ref)

    for book in range(2):
        bins_ref[book] += totals[book]


def bin_gradients(attended, misfit, codes, scales, scaling):
    steps, tokens, width = attended.shape
    blocks, groups, rows = codes.shape
    return pl.pallas_call(
        lambda *refs: bins_kernel(scaling, *refs),
        grid=(blocks,),
        in_specs=[
            pl.BlockSpec((steps, tokens, width), lambda i: (0, 0, 0)),
            pl.BlockSpec((tokens, rows), lambda i: (0, i)),
            pl.BlockSpec((None, groups, rows), lambda i: (i, 0, 0)),
            pl.BlockSpec((None, 1, rows), lambda i: (i, 0, 0)),
        ],
        out_specs=pl.BlockSpec((2, HIGH, LOW * GROUP), lambda i: (0, 0, 0)),
        out_shape=jax.ShapeDtypeStruct((2, HIGH, LOW * GROUP), f32),
        scratch_shapes=[
            pltpu.VMEM((steps * width, rows), f32),
            pltpu.VMEM((4, groups, rows), f32),
        ],
        cost_estimate=pl.CostEstimate(
            flops=blocks * 8_000_000_000, transcendentals=0, bytes_accessed=blocks * 2_000_000
        ),
        name="bins",
    )(attended, misfit, codes, scales)


def attend(queries, keys, values, places):
    scores = jnp.einsum("qd,kd->qk", queries, keys, preferred_element_type=f32) / math.sqrt(HEAD_DIM)
    allowed = lax.iota(jnp.int32, keys.shape[0])[None, :] <= places[:, None]
    row_max = jnp.max(jnp.where(allowed, scores, -1e30), axis=-1, keepdims=True)
    exponent = jnp.where(allowed, jnp.exp(scores - row_max), 0.0)
    row_sum = jnp.sum(exponent, axis=-1, keepdims=True)
    weighted = jnp.einsum("qk,kd->qd", exponent.astype(bf16), values, preferred_element_type=f32)
    return (weighted / row_sum).astype(bf16)


def device_part(
    queries, key_rows, values, code_first, code_second, book_first, book_second, scales, target
):
    tok_rows, _ = queries.shape
    high, across = lax.axis_index("tok_0"), lax.axis_index("tok_1")
    count_across = lax.axis_size("tok_1")
    lane, core = lax.axis_index("col_0"), lax.axis_index("col_1")
    count_lane = lax.axis_size("col_0")
    rows = code_first.shape[0]
    tokens = lax.axis_size(TOK) * tok_rows

    def of_head(array, head):
        return lax.dynamic_slice_in_dim(array, head * HEAD_DIM, HEAD_DIM, 1)

    their_queries = swap(of_head(queries, 1 - high), "tok_0")
    pairs = jnp.stack(
        [jnp.concatenate([of_head(key_rows, h), of_head(values, h)], axis=1) for h in range(2)]
    )
    pairs = jnp.broadcast_to(pairs[:, None], (2, count_across, tok_rows, 2 * HEAD_DIM))
    pairs = exchange(pairs.reshape(-1, tok_rows, 2 * HEAD_DIM), TOK)
    pairs = pairs.reshape(tokens, 2 * HEAD_DIM)
    own_queries = jnp.concatenate(in_order(of_head(queries, high), their_queries, high), axis=0)
    place = across * tok_rows + lax.iota(jnp.int32, tok_rows)
    places = jnp.concatenate([place, place + count_across * tok_rows])
    head_out = attend(own_queries, pairs[:, :HEAD_DIM], pairs[:, HEAD_DIM:], places)
    head_out = jnp.concatenate(in_order(head_out, swap(head_out, "tok_0"), high), axis=1)
    attended = copies(head_out, "row")

    own_codes = (code_first + ENTRIES * code_second).T.astype(f32)
    share = tok_rows // count_lane
    wanted = target.reshape(2, count_across, count_lane, share, rows)
    wanted = lax.dynamic_index_in_dim(wanted, core, 0, keepdims=False)
    wanted = lax.dynamic_index_in_dim(wanted, lane, 1, keepdims=False).astype(f32)
    groups = own_codes.shape[0]
    own_scales = jnp.broadcast_to(scales[None, None], (count_across, 8, rows))
    sent = jnp.broadcast_to(own_codes[None], (count_across, groups, rows))
    sent = jnp.concatenate([sent, own_scales, wanted], axis=1)
    sent, _ = lax.optimization_barrier((sent, pairs))
    side = exchange(sent, "tok_1")
    codes, row_scales, wanted = side[:, :groups], side[:, groups : groups + 1], side[:, groups + 8 :]
    books = jnp.stack([book_first, book_second]).astype(f32).transpose(0, 2, 1)
    table = books.reshape(2, GROUP, 2, 128).transpose(0, 2, 1, 3).reshape(4, GROUP, 128)
    own_weight = dequantize(own_codes[None], table, scales[None, None])
    following = (across + 1 + lax.iota(jnp.int32, count_across - 1)) % count_across
    other_codes = [lax.dynamic_slice_in_dim(codes, following[k], 1, 0) for k in range(3)]
    other_scales = [lax.dynamic_slice_in_dim(row_scales, following[k], 1, 0) for k in range(3)]
    other_codes, other_scales = jnp.concatenate(other_codes), jnp.concatenate(other_scales)
    other_weight = dequantize(other_codes, table, other_scales)

    keep, send = project(jnp.stack([across, core]), attended, own_weight, other_weight)
    half_sum = (keep + swap(send, "col_1")).astype(bf16)
    parts = exchange(half_sum.reshape(count_lane, share, -1), "col_0")
    output = jnp.sum(parts.astype(f32), axis=0)
    wanted = wanted.transpose(1, 0, 2).reshape(share, -1)
    misfit_share = (output - wanted).astype(bf16)
    misfit_half = copies(misfit_share, "col_0").reshape(tok_rows, -1)
    other_half = swap(misfit_half, "col_1")
    misfit = jnp.concatenate(in_order(misfit_half, other_half, core), axis=0)

    by_rows = misfit.reshape(2 * tok_rows, count_across, rows).transpose(1, 0, 2)
    by_tokens = exchange(by_rows, "tok_1").reshape(count_across, 2, tok_rows, rows)

    scale_part = jnp.sum(misfit_share.astype(f32) * output, axis=0).reshape(count_across, rows)
    scale_part = scale_part / (row_scales[:, 0] * tokens)
    bins = bin_gradients(attended, misfit, codes, row_scales, 1.0 / tokens)

    peers = COL + ("tok_1",)
    count_col = lax.axis_size(COL)
    scale_part = scale_part.reshape(count_across, count_col, -1).transpose(1, 0, 2)
    piece = scale_part.shape[2]
    scale_part = scale_part.reshape(count_col * count_across, 1, piece)
    bins = bins.reshape(count_col * count_across, 1, 128)
    scale_part = jnp.pad(scale_part, ((0, 0), (0, 0), (0, 128 - piece)))
    sums = jnp.concatenate([bins, scale_part], axis=1)
    sums, by_tokens = lax.optimization_barrier((sums, by_tokens))
    sums = jnp.sum(exchange(sums, peers), axis=0)
    bins = jnp.sum(copies(sums[:1], ("row", "tok_0")), axis=0)
    done = copies(jnp.concatenate([bins, sums[1:]], axis=0), peers)
    grad_scales = done[:, 1, :piece].reshape(count_col, count_across, piece)
    grad_scales = lax.dynamic_index_in_dim(grad_scales, across, 1, keepdims=False).reshape(rows)
    misfit_out = by_tokens.transpose(1, 0, 2, 3).reshape(tokens, rows)
    return misfit_out, grad_scales, done[:, 0].reshape(2, ENTRIES, GROUP)


def solution(mesh):
    split = Mesh(
        mesh.devices.reshape(4, 2, mesh.shape["row"], 2, 4),
        ("col_0", "col_1", "row", "tok_0", "tok_1"),
    )
    return jax.shard_map(
        device_part,
        mesh=split,
        in_specs=(
            P(TOK, COL_ROW),
            P(TOK, COL_ROW),
            P(TOK, COL_ROW),
            P(ROW_TOK, COL),
            P(ROW_TOK, COL),
            P(),
            P(),
            P(ROW_TOK),
            P(None, ROW_TOK),
        ),
        out_specs=(P(None, ROW_TOK), P(ROW_TOK), P()),
        check_vma=False,
    )
```

```python
import math

import jax
import jax.numpy as jnp
from jax import lax
from jax.experimental import pallas as pl
from jax.experimental.pallas import tpu as pltpu
from jax.sharding import Mesh
from jax.sharding import PartitionSpec as P


HEAD_DIM = 128
ENTRIES = 256
GROUP = 8
LOW = 8
HIGH = ENTRIES // LOW
TOK = ("tok_0", "tok_1")
ROW_TOK = ("row", "tok_0", "tok_1")
COL = ("col_0", "col_1")
COL_ROW = ("col_0", "col_1", "row")
f32, bf16 = jnp.float32, jnp.bfloat16


def exchange(pieces, axis):
    return lax.all_to_all(pieces, axis, 0, 0, tiled=True)


def copies(array, axis):
    pieces = jnp.broadcast_to(array[None], (lax.axis_size(axis), *array.shape))
    return exchange(pieces, axis)


def swap(array, axis):
    return lax.ppermute(array, axis, [(0, 1), (1, 0)])


def in_order(mine, theirs, place):
    first = place == 0
    return jnp.where(first, mine, theirs), jnp.where(first, theirs, mine)


def dequant_kernel(block_ref, table_ref, *refs):
    weight_ref, plan_ref = refs[-2:]
    groups, rows = weight_ref.shape[0] // GROUP, weight_ref.shape[1]
    tables = [table_ref[i] for i in range(4)]
    plan_ref[...] = block_ref[: groups + 8, :]
    scale = jnp.broadcast_to(block_ref[groups : groups + 1, :], (GROUP, rows))

    def group_rows(g):
        both = jnp.broadcast_to(block_ref[pl.ds(g, 1), :], (GROUP, rows)).astype(jnp.int32)
        parts = []
        for at in range(0, rows, 128):
            packed = both[:, at : at + 128]
            total = None
            for book in range(2):
                code = (packed & 255) if book == 0 else (packed >> 8)
                place = code & 127
                near = jnp.take_along_axis(tables[2 * book], place, axis=1)
                far = jnp.take_along_axis(tables[2 * book + 1], place, axis=1)
                entry = jnp.where(code >= 128, far, near)
                total = entry if total is None else total + entry
            parts.append(total * scale[:, at : at + 128])
        return jnp.concatenate(parts, axis=1)

    def step(i, carry):
        for k in range(4):
            pair = [group_rows(i * 8 + 2 * k + n) for n in range(2)]
            start = pl.multiple_of(i * 64 + 16 * k, 16)
            weight_ref[pl.ds(start, 16), :] = jnp.concatenate(pair, axis=0).astype(bf16)
        return carry

    lax.fori_loop(0, groups // 8, step, 0)


def dequantize(block, table, at, blocks, groups, before=()):
    rows = block.shape[1]
    return pl.pallas_call(
        dequant_kernel,
        grid=(1,),
        in_specs=[
            pl.BlockSpec(block.shape, lambda i: (0, 0)),
            pl.BlockSpec((4, GROUP, 128), lambda i: (0, 0, 0)),
        ]
        + [pl.BlockSpec(memory_space=pl.ANY)] * len(before),
        out_specs=[
            pl.BlockSpec((None, groups * GROUP, rows), lambda i: (at, 0, 0)),
            pl.BlockSpec((None, groups + 8, rows), lambda i: (at, 0, 0)),
        ],
        out_shape=[
            jax.ShapeDtypeStruct((blocks, groups * GROUP, rows), bf16),
            jax.ShapeDtypeStruct((blocks, groups + 8, rows), f32),
        ],
        input_output_aliases={2: 0, 3: 1} if before else {},
        cost_estimate=pl.CostEstimate(
            flops=8_000_000_000, transcendentals=0, bytes_accessed=1_500_000
        ),
        name="dequant",
    )(block, table, *before)


def project_kernel(place_ref, att_ref, weight_ref, keep_ref, send_ref, all_ref):
    steps, tokens, width = att_ref.shape
    half = tokens // 2
    total = None
    for z in range(steps):
        part = jnp.dot(
            att_ref[z], weight_ref[z * width : (z + 1) * width, :], preferred_element_type=f32
        )
        total = part if total is None else total + part
    all_ref[...] = total
    keep_ref[...] = all_ref[pl.ds(pl.multiple_of(place_ref[1] * half, half), half), :]
    send_ref[...] = all_ref[pl.ds(pl.multiple_of((1 - place_ref[1]) * half, half), half), :]


def project(place, attended, weight):
    steps, tokens, width = attended.shape
    blocks, depth, rows = weight.shape
    out = jax.ShapeDtypeStruct((tokens // 2, blocks * rows), f32)
    out_spec = pl.BlockSpec((tokens // 2, rows), lambda i, place: (0, (place[0] + i) % blocks))
    return pl.pallas_call(
        project_kernel,
        grid_spec=pltpu.PrefetchScalarGridSpec(
            num_scalar_prefetch=1,
            grid=(blocks,),
            in_specs=[
                pl.BlockSpec((steps, tokens, width), lambda i, place: (0, 0, 0)),
                pl.BlockSpec((None, depth, rows), lambda i, place: (i, 0, 0)),
            ],
            out_specs=[out_spec, out_spec],
            scratch_shapes=[pltpu.VMEM((tokens, rows), f32)],
        ),
        out_shape=[out, out],
        name="project",
    )(place, attended, weight)


def bins_kernel(scaling, place_ref, att_ref, misfit_ref, plan_ref, bins_ref, grad_ref, digit_ref):
    groups, rows = digit_ref.shape[1:]
    steps, _, width = att_ref.shape
    scale = plan_ref[groups : groups + 1, :] * scaling
    misfit = misfit_ref[...]
    for z in range(steps):
        weight_grad = lax.dot_general(
            att_ref[z], misfit, (((0,), (0,)), ((), ())), preferred_element_type=f32
        )
        grad_ref[z * width : (z + 1) * width, :] = weight_grad * scale
    packed = plan_ref[:groups, :].astype(jnp.int32)
    for book in range(2):
        code = (packed & 255) if book == 0 else (packed >> 8)
        digit_ref[2 * book] = (code & (LOW - 1)).astype(f32)
        digit_ref[2 * book + 1] = (code >> 3).astype(f32)
    at = lax.broadcasted_iota(jnp.int32, (16, rows), 0)
    low_rows = [(2 * d + (at >= 8).astype(jnp.int32)).astype(f32).astype(bf16) for d in range(LOW // 2)]
    high_rows = [(16 * d + at).astype(f32).astype(bf16) for d in range(HIGH // 16)]
    zero, one = jnp.zeros((16, rows), bf16), jnp.ones((16, rows), bf16)
    chunk = 8

    def digit(which, g):
        return jnp.broadcast_to(digit_ref[which, pl.ds(g, 1), :], (16, rows)).astype(bf16)

    def step(i, totals):
        twice = []
        for k in range(chunk):
            entry = grad_ref[pl.ds(pl.multiple_of((i * chunk + k) * GROUP, GROUP), GROUP), :]
            twice.append(jnp.concatenate([entry, entry], axis=0).astype(bf16))
        done = []
        for book in range(2):
            highs, lows = [], []
            for k in range(chunk):
                low, high = digit(2 * book, i * chunk + k), digit(2 * book + 1, i * chunk + k)
                lows.append(
                    jnp.concatenate([jnp.where(low == r, twice[k], zero) for r in low_rows], axis=0)
                )
                highs.append(
                    jnp.concatenate([jnp.where(high == r, one, zero) for r in high_rows], axis=0)
                )
            part = lax.dot_general(
                jnp.concatenate(highs, axis=1),
                jnp.concatenate(lows, axis=1),
                (((1,), (1,)), ((), ())),
                preferred_element_type=f32,
            )
            done.append(totals[book] + part)
        return tuple(done)

    empty = jnp.zeros((HIGH, LOW * GROUP), f32)
    totals = lax.fori_loop(0, groups // chunk, step, (empty, empty), unroll=2)

    @pl.when(pl.program_id(0) == 0)
    def _():
        bins_ref[...] = jnp.zeros_like(bins_ref)

    for book in range(2):
        bins_ref[book] += totals[book]


def bin_gradients(place, attended, misfit, plan, scaling):
    steps, tokens, width = attended.shape
    blocks, depth, rows = plan.shape
    return pl.pallas_call(
        lambda *refs: bins_kernel(scaling, *refs),
        grid_spec=pltpu.PrefetchScalarGridSpec(
            num_scalar_prefetch=1,
            grid=(blocks,),
            in_specs=[
                pl.BlockSpec((steps, tokens, width), lambda i, place: (0, 0, 0)),
                pl.BlockSpec((tokens, rows), lambda i, place: (0, (place[0] + i) % blocks)),
                pl.BlockSpec((None, depth, rows), lambda i, place: (i, 0, 0)),
            ],
            out_specs=pl.BlockSpec((2, HIGH, LOW * GROUP), lambda i, place: (0, 0, 0)),
            scratch_shapes=[
                pltpu.VMEM((steps * width, rows), f32),
                pltpu.VMEM((4, depth - 8, rows), f32),
            ],
        ),
        out_shape=jax.ShapeDtypeStruct((2, HIGH, LOW * GROUP), f32),
        cost_estimate=pl.CostEstimate(
            flops=blocks * 8_000_000_000, transcendentals=0, bytes_accessed=blocks * 2_000_000
        ),
        name="bins",
    )(place, attended, misfit, plan)


def attend(queries, keys, values, query_places, key_places):
    scores = jnp.einsum("qd,kd->qk", queries, keys, preferred_element_type=f32) / math.sqrt(HEAD_DIM)
    allowed = key_places[None, :] <= query_places[:, None]
    row_max = jnp.max(jnp.where(allowed, scores, -1e30), axis=-1, keepdims=True)
    exponent = jnp.where(allowed, jnp.exp(scores - row_max), 0.0)
    row_sum = jnp.sum(exponent, axis=-1, keepdims=True)
    weighted = jnp.einsum("qk,kd->qd", exponent.astype(bf16), values, preferred_element_type=f32)
    return (weighted / row_sum).astype(bf16)


def device_part(
    queries, key_rows, values, code_first, code_second, book_first, book_second, scales, target
):
    tok_rows, _ = queries.shape
    high, across = lax.axis_index("tok_0"), lax.axis_index("tok_1")
    count_across = lax.axis_size("tok_1")
    lane, core = lax.axis_index("col_0"), lax.axis_index("col_1")
    count_lane, count_col = lax.axis_size("col_0"), lax.axis_size(COL)
    rows = code_first.shape[0]
    tokens = lax.axis_size(TOK) * tok_rows

    def of_head(head):
        picked = [
            lax.dynamic_slice_in_dim(array, head * HEAD_DIM, HEAD_DIM, 1)
            for array in (queries, key_rows, values)
        ]
        return jnp.concatenate(picked, axis=1)

    mine = of_head(high)
    both = jnp.concatenate(in_order(mine, swap(of_head(1 - high), "tok_0"), high))
    pairs = copies(both[:, HEAD_DIM:], "tok_1")
    block = lax.iota(jnp.int32, 2)[:, None] * (count_across * tok_rows)
    block = block + lax.iota(jnp.int32, tok_rows)[None, :]
    query_places = (block + across * tok_rows).reshape(-1)
    key_places = lax.iota(jnp.int32, count_across)[:, None, None] * tok_rows + block[None]
    pairs = pairs.reshape(tokens, 2 * HEAD_DIM)
    head_out = attend(
        both[:, :HEAD_DIM], pairs[:, :HEAD_DIM], pairs[:, HEAD_DIM:], query_places, key_places.reshape(-1)
    )
    other_out = swap(head_out, "tok_0")
    attended = copies(jnp.concatenate(in_order(head_out, other_out, high), axis=1), "row")

    own_codes = (code_first + ENTRIES * code_second).T.astype(f32)
    groups = own_codes.shape[0]
    share = tok_rows // count_lane
    wanted = target.reshape(2, count_across, count_lane, share, rows)
    wanted = lax.dynamic_index_in_dim(wanted, core, 0, keepdims=False)
    wanted = lax.dynamic_index_in_dim(wanted, lane, 1, keepdims=False).astype(f32)
    own_scales = jnp.broadcast_to(scales[None], (8, rows))

    def block_for(peer):
        part = lax.dynamic_index_in_dim(wanted, peer, 0, keepdims=False)
        return jnp.concatenate([own_codes, own_scales, part], axis=0)

    own_block = block_for(across)
    books = jnp.stack([book_first, book_second]).astype(f32).transpose(0, 2, 1)
    table = books.reshape(2, GROUP, 2, 128).transpose(0, 2, 1, 3).reshape(4, GROUP, 128)
    received = [own_block]
    built = dequantize(own_block, table, 0, count_across, groups)
    for k in range(1, count_across):
        sent, _ = lax.optimization_barrier((block_for((across + count_across - k) % count_across), pairs))
        route = [((i + k) % count_across, i) for i in range(count_across)]
        received.append(lax.ppermute(sent, "tok_1", route))
        built = dequantize(received[k], table, k, count_across, groups, built)
    weight, plan = built

    place = jnp.stack([across, core])
    keep, send = project(place, attended, weight)
    half_sum = (keep + swap(send, "col_1")).astype(bf16)
    parts = exchange(half_sum.reshape(count_lane, share, -1), "col_0")
    output = jnp.sum(parts.astype(f32), axis=0)
    wanted = jnp.stack([block[groups + 8 :] for block in received] * 2)
    wanted = lax.dynamic_slice_in_dim(wanted, (count_across - across) % count_across, count_across, 0)
    wanted = wanted.transpose(1, 0, 2).reshape(share, -1)
    misfit_share = (output - wanted).astype(bf16)
    misfit_half = copies(misfit_share, "col_0").reshape(tok_rows, -1)
    other_half = swap(misfit_half, "col_1")
    misfit = jnp.concatenate(in_order(misfit_half, other_half, core), axis=0)

    by_rows = misfit.reshape(2 * tok_rows, count_across, rows).transpose(1, 0, 2)
    by_tokens = exchange(by_rows, "tok_1").reshape(count_across, 2, tok_rows, rows)

    scale_part = jnp.sum(misfit_share.astype(f32) * output, axis=0).reshape(count_across, -1, 128)
    extra = scale_part.shape[1]
    bins = bin_gradients(place, attended, misfit, plan, 1.0 / tokens)

    bins = jnp.broadcast_to(bins.reshape(1, -1, 128), (count_across, 2 * ENTRIES * GROUP // 128, 128))
    sums = jnp.concatenate([bins, scale_part], axis=1)
    sums, by_tokens = lax.optimization_barrier((sums, by_tokens))
    sums = jnp.sum(exchange(sums, "tok_1"), axis=0)
    upper = sums.astype(bf16)
    lower = (sums[-extra:] - upper[-extra:].astype(f32)).astype(bf16)
    sums = copies(jnp.concatenate([upper, lower]), COL + ("tok_0",)).astype(f32)
    scale_sums = lax.dynamic_index_in_dim(sums.reshape(count_col, 2, -1, 128), high, 1, keepdims=False)
    scale_sums = jnp.sum(scale_sums[:, -2 * extra :], axis=0)
    scale_sums = (scale_sums[:extra] + scale_sums[extra:]).reshape(rows)
    bins = jnp.sum(sums[:, : -2 * extra], axis=0).astype(bf16)
    bins = jnp.sum(copies(bins, "row").astype(f32), axis=0)
    misfit_out = by_tokens.transpose(1, 0, 2, 3).reshape(tokens, rows)
    return misfit_out, scale_sums / (scales * tokens), bins.reshape(2, ENTRIES, GROUP)


def solution(mesh):
    split = Mesh(
        mesh.devices.reshape(4, 2, mesh.shape["row"], 2, 4),
        ("col_0", "col_1", "row", "tok_0", "tok_1"),
    )
    return jax.shard_map(
        device_part,
        mesh=split,
        in_specs=(
            P(TOK, COL_ROW),
            P(TOK, COL_ROW),
            P(TOK, COL_ROW),
            P(ROW_TOK, COL),
            P(ROW_TOK, COL),
            P(),
            P(),
            P(ROW_TOK),
            P(None, ROW_TOK),
        ),
        out_specs=(P(None, ROW_TOK), P(ROW_TOK), P()),
        check_vma=False,
    )
```

```python
import math

import jax
import jax.numpy as jnp
from jax import lax
from jax.experimental import pallas as pl
from jax.experimental.pallas import tpu as pltpu
from jax.sharding import Mesh
from jax.sharding import PartitionSpec as P


HEAD_DIM = 128
ENTRIES = 256
GROUP = 8
LOW = 8
HIGH = ENTRIES // LOW
TOK = ("tok_0", "tok_1")
ROW_TOK = ("row", "tok_0", "tok_1")
COL = ("col_0", "col_1")
COL_ROW = ("col_0", "col_1", "row")
f32, bf16 = jnp.float32, jnp.bfloat16


def exchange(pieces, axis):
    return lax.all_to_all(pieces, axis, 0, 0, tiled=True)


def copies(array, axis):
    pieces = jnp.broadcast_to(array[None], (lax.axis_size(axis), *array.shape))
    return exchange(pieces, axis)


def swap(array, axis):
    return lax.ppermute(array, axis, [(0, 1), (1, 0)])


def in_order(mine, theirs, place):
    first = place == 0
    return jnp.where(first, mine, theirs), jnp.where(first, theirs, mine)


def dequant_kernel(block_ref, first_ref, second_ref, *refs):
    weight_ref, plan_ref, digit_ref = refs[-3:]
    groups, rows = weight_ref.shape[0] // GROUP, weight_ref.shape[1]
    tables, by_digit = [], []
    lanes = lax.broadcasted_iota(jnp.int32, (GROUP, 128), 1)
    for book_ref in (first_ref, second_ref):
        halves = [book_ref[:, start : start + 128].astype(f32) for start in (0, 128)]
        tables += halves
        digit_rows = []
        for d in range(LOW):
            place = (lanes * LOW + d) & 127
            near, far = (
                jnp.take_along_axis(half, place, axis=1, mode="promise_in_bounds") for half in halves
            )
            digit_rows.append(jnp.where(lanes < 128 // LOW, near, far))
        by_digit.append(jnp.concatenate(digit_rows, axis=0)[:, :HIGH].astype(bf16))
    plan_ref[...] = block_ref[: groups + 8, :]
    scale = jnp.broadcast_to(block_ref[groups : groups + 1, :], (GROUP, rows))
    packed = block_ref[:groups, :].astype(jnp.int32)
    for book in range(2):
        code = (packed & 255) if book == 0 else (packed >> 8)
        digit_ref[2 * book] = (code & (LOW - 1)).astype(f32)
        digit_ref[2 * book + 1] = (code >> 3).astype(f32)
    at = lax.broadcasted_iota(jnp.int32, (16, rows), 0)
    high_rows = [(16 * d + at).astype(f32).astype(bf16) for d in range(HIGH // 16)]
    zero, one = jnp.zeros((16, rows), bf16), jnp.ones((16, rows), bf16)

    def picked(book, half, place):
        return jnp.take_along_axis(tables[2 * book + half], place, axis=1, mode="promise_in_bounds")

    def by_gather(g):
        both = jnp.broadcast_to(block_ref[pl.ds(g, 1), :], (GROUP, rows)).astype(jnp.int32)
        parts = []
        for start in range(0, rows, 128):
            packed = both[:, start : start + 128]
            total = None
            for book in range(2):
                code = (packed & 255) if book == 0 else (packed >> 8)
                place = code & 127
                entry = jnp.where(code >= 128, picked(book, 1, place), picked(book, 0, place))
                total = entry if total is None else total + entry
            parts.append(total * scale[:, start : start + 128])
        return jnp.concatenate(parts, axis=1)

    def by_product(g):
        total = None
        for book in range(2):
            high = jnp.broadcast_to(digit_ref[2 * book + 1, pl.ds(g, 1), :], (16, rows)).astype(bf16)
            hot = jnp.concatenate([jnp.where(high == r, one, zero) for r in high_rows], axis=0)
            near = jnp.dot(by_digit[book], hot, preferred_element_type=f32)
            low = jnp.broadcast_to(digit_ref[2 * book, pl.ds(g, 1), :], (GROUP, rows))
            entry = near[:GROUP]
            for d in range(1, LOW):
                entry = jnp.where(low == float(d), near[d * GROUP : (d + 1) * GROUP], entry)
            total = entry if total is None else total + entry
        return total * scale

    chunk = 16

    def step(i, carry):
        for k in range(0, chunk, 2):
            g = i * chunk + k
            pair = jnp.concatenate([by_gather(g), by_product(g + 1)], axis=0)
            weight_ref[pl.ds(pl.multiple_of(g * GROUP, 16), 16), :] = pair.astype(bf16)
        return carry

    lax.fori_loop(0, groups // chunk, step, 0, unroll=2)


def dequantize(block, books, at, blocks, groups, before=()):
    rows = block.shape[1]
    return pl.pallas_call(
        dequant_kernel,
        grid=(1,),
        in_specs=[
            pl.BlockSpec(block.shape, lambda i: (0, 0)),
            pl.BlockSpec(books[0].shape, lambda i: (0, 0)),
            pl.BlockSpec(books[1].shape, lambda i: (0, 0)),
        ]
        + [pl.BlockSpec(memory_space=pl.ANY)] * len(before),
        out_specs=[
            pl.BlockSpec((None, groups * GROUP, rows), lambda i: (at, 0, 0)),
            pl.BlockSpec((None, groups + 8, rows), lambda i: (at, 0, 0)),
        ],
        out_shape=[
            jax.ShapeDtypeStruct((blocks, groups * GROUP, rows), bf16),
            jax.ShapeDtypeStruct((blocks, groups + 8, rows), f32),
        ],
        scratch_shapes=[pltpu.VMEM((4, groups, rows), f32)],
        input_output_aliases={3: 0, 4: 1} if before else {},
        cost_estimate=pl.CostEstimate(
            flops=8_000_000_000, transcendentals=0, bytes_accessed=1_500_000
        ),
        name="dequant",
    )(block, *books, *before)


def project_kernel(place_ref, att_ref, weight_ref, keep_ref, send_ref, all_ref):
    steps, tokens, width = att_ref.shape
    half = tokens // 2
    total = None
    for z in range(steps):
        part = jnp.dot(
            att_ref[z], weight_ref[z * width : (z + 1) * width, :], preferred_element_type=f32
        )
        total = part if total is None else total + part
    all_ref[...] = total
    keep_ref[...] = all_ref[pl.ds(pl.multiple_of(place_ref[1] * half, half), half), :]
    send_ref[...] = all_ref[pl.ds(pl.multiple_of((1 - place_ref[1]) * half, half), half), :]


def project(place, attended, weight):
    steps, tokens, width = attended.shape
    blocks, depth, rows = weight.shape
    out = jax.ShapeDtypeStruct((tokens // 2, blocks * rows), f32)
    out_spec = pl.BlockSpec((tokens // 2, rows), lambda i, place: (0, (place[0] + i) % blocks))
    return pl.pallas_call(
        project_kernel,
        grid_spec=pltpu.PrefetchScalarGridSpec(
            num_scalar_prefetch=1,
            grid=(blocks,),
            in_specs=[
                pl.BlockSpec((steps, tokens, width), lambda i, place: (0, 0, 0)),
                pl.BlockSpec((None, depth, rows), lambda i, place: (i, 0, 0)),
            ],
            out_specs=[out_spec, out_spec],
            scratch_shapes=[pltpu.VMEM((tokens, rows), f32)],
        ),
        out_shape=[out, out],
        name="project",
    )(place, attended, weight)


def bins_kernel(scaling, place_ref, att_ref, misfit_ref, plan_ref, bins_ref, grad_ref, digit_ref):
    groups, rows = digit_ref.shape[1:]
    steps, _, width = att_ref.shape
    scale = plan_ref[groups : groups + 1, :] * scaling
    misfit = misfit_ref[...]
    for z in range(steps):
        weight_grad = lax.dot_general(
            att_ref[z], misfit, (((0,), (0,)), ((), ())), preferred_element_type=f32
        )
        grad_ref[z * width : (z + 1) * width, :] = weight_grad * scale
    packed = plan_ref[:groups, :].astype(jnp.int32)
    for book in range(2):
        code = (packed & 255) if book == 0 else (packed >> 8)
        digit_ref[2 * book] = (code & (LOW - 1)).astype(f32)
        digit_ref[2 * book + 1] = (code >> 3).astype(f32)
    at = lax.broadcasted_iota(jnp.int32, (16, rows), 0)
    low_rows = [(2 * d + (at >= 8).astype(jnp.int32)).astype(f32).astype(bf16) for d in range(LOW // 2)]
    high_rows = [(16 * d + at).astype(f32).astype(bf16) for d in range(HIGH // 16)]
    zero, one = jnp.zeros((16, rows), bf16), jnp.ones((16, rows), bf16)
    chunk = 8

    def digit(which, g):
        return jnp.broadcast_to(digit_ref[which, pl.ds(g, 1), :], (16, rows)).astype(bf16)

    def step(i, totals):
        twice = []
        for k in range(chunk):
            entry = grad_ref[pl.ds(pl.multiple_of((i * chunk + k) * GROUP, GROUP), GROUP), :]
            twice.append(jnp.concatenate([entry, entry], axis=0).astype(bf16))
        done = []
        for book in range(2):
            highs, lows = [], []
            for k in range(chunk):
                low, high = digit(2 * book, i * chunk + k), digit(2 * book + 1, i * chunk + k)
                lows.append(
                    jnp.concatenate([jnp.where(low == r, twice[k], zero) for r in low_rows], axis=0)
                )
                highs.append(
                    jnp.concatenate([jnp.where(high == r, one, zero) for r in high_rows], axis=0)
                )
            part = lax.dot_general(
                jnp.concatenate(highs, axis=1),
                jnp.concatenate(lows, axis=1),
                (((1,), (1,)), ((), ())),
                preferred_element_type=f32,
            )
            done.append(totals[book] + part)
        return tuple(done)

    empty = jnp.zeros((HIGH, LOW * GROUP), f32)
    totals = lax.fori_loop(0, groups // chunk, step, (empty, empty), unroll=2)

    @pl.when(pl.program_id(0) == 0)
    def _():
        bins_ref[...] = jnp.zeros_like(bins_ref)

    for book in range(2):
        bins_ref[book] += totals[book]


def bin_gradients(place, attended, misfit, plan, scaling):
    steps, tokens, width = attended.shape
    blocks, depth, rows = plan.shape
    return pl.pallas_call(
        lambda *refs: bins_kernel(scaling, *refs),
        grid_spec=pltpu.PrefetchScalarGridSpec(
            num_scalar_prefetch=1,
            grid=(blocks,),
            in_specs=[
                pl.BlockSpec((steps, tokens, width), lambda i, place: (0, 0, 0)),
                pl.BlockSpec((tokens, rows), lambda i, place: (0, (place[0] + i) % blocks)),
                pl.BlockSpec((None, depth, rows), lambda i, place: (i, 0, 0)),
            ],
            out_specs=pl.BlockSpec((2, HIGH, LOW * GROUP), lambda i, place: (0, 0, 0)),
            scratch_shapes=[
                pltpu.VMEM((steps * width, rows), f32),
                pltpu.VMEM((4, depth - 8, rows), f32),
            ],
        ),
        out_shape=jax.ShapeDtypeStruct((2, HIGH, LOW * GROUP), f32),
        cost_estimate=pl.CostEstimate(
            flops=blocks * 8_000_000_000, transcendentals=0, bytes_accessed=blocks * 2_000_000
        ),
        name="bins",
    )(place, attended, misfit, plan)


def attend(queries, keys, values, query_places, key_places):
    scores = jnp.einsum("qd,kd->qk", queries, keys, preferred_element_type=f32) / math.sqrt(HEAD_DIM)
    allowed = key_places[None, :] <= query_places[:, None]
    row_max = jnp.max(jnp.where(allowed, scores, -1e30), axis=-1, keepdims=True)
    exponent = jnp.where(allowed, jnp.exp(scores - row_max), 0.0)
    row_sum = jnp.sum(exponent, axis=-1, keepdims=True)
    weighted = jnp.einsum("qk,kd->qd", exponent.astype(bf16), values, preferred_element_type=f32)
    return (weighted / row_sum).astype(bf16)


def device_part(
    queries, key_rows, values, code_first, code_second, book_first, book_second, scales, target
):
    tok_rows, _ = queries.shape
    high, across = lax.axis_index("tok_0"), lax.axis_index("tok_1")
    count_across = lax.axis_size("tok_1")
    lane, core = lax.axis_index("col_0"), lax.axis_index("col_1")
    count_lane, count_col = lax.axis_size("col_0"), lax.axis_size(COL)
    rows = code_first.shape[0]
    tokens = lax.axis_size(TOK) * tok_rows

    def of_head(head):
        picked = [
            lax.dynamic_slice_in_dim(array, head * HEAD_DIM, HEAD_DIM, 1)
            for array in (queries, key_rows, values)
        ]
        return jnp.concatenate(picked, axis=1)

    mine = of_head(high)
    both = jnp.concatenate(in_order(mine, swap(of_head(1 - high), "tok_0"), high))
    pairs = copies(both[:, HEAD_DIM:], "tok_1")
    block = lax.iota(jnp.int32, 2)[:, None] * (count_across * tok_rows)
    block = block + lax.iota(jnp.int32, tok_rows)[None, :]
    query_places = (block + across * tok_rows).reshape(-1)
    key_places = lax.iota(jnp.int32, count_across)[:, None, None] * tok_rows + block[None]
    pairs = pairs.reshape(tokens, 2 * HEAD_DIM)
    head_out = attend(
        both[:, :HEAD_DIM], pairs[:, :HEAD_DIM], pairs[:, HEAD_DIM:], query_places, key_places.reshape(-1)
    )
    other_out = swap(head_out, "tok_0")
    attended = copies(jnp.concatenate(in_order(head_out, other_out, high), axis=1), "row")

    own_codes = (code_first + ENTRIES * code_second).T.astype(f32)
    groups = own_codes.shape[0]
    share = tok_rows // count_lane
    wanted = target.reshape(2, count_across, count_lane, share, rows)
    wanted = lax.dynamic_index_in_dim(wanted, core, 0, keepdims=False)
    wanted = lax.dynamic_index_in_dim(wanted, lane, 1, keepdims=False).astype(f32)
    own_scales = jnp.broadcast_to(scales[None], (8, rows))

    def block_for(peer):
        part = lax.dynamic_index_in_dim(wanted, peer, 0, keepdims=False)
        return jnp.concatenate([own_codes, own_scales, part], axis=0)

    own_block = block_for(across)
    books = (book_first.T, book_second.T)
    received = [own_block]
    built = dequantize(own_block, books, 0, count_across, groups)
    for k in range(1, count_across):
        sent, _ = lax.optimization_barrier((block_for((across + count_across - k) % count_across), pairs))
        route = [((i + k) % count_across, i) for i in range(count_across)]
        received.append(lax.ppermute(sent, "tok_1", route))
        built = dequantize(received[k], books, k, count_across, groups, built)
    weight, plan = built

    place = jnp.stack([across, core])
    keep, send = project(place, attended, weight)
    half_sum = (keep + swap(send, "col_1")).astype(bf16)
    parts = exchange(half_sum.reshape(count_lane, share, -1), "col_0")
    output = jnp.sum(parts.astype(f32), axis=0)
    wanted = jnp.stack([block[groups + 8 :] for block in received] * 2)
    wanted = lax.dynamic_slice_in_dim(wanted, (count_across - across) % count_across, count_across, 0)
    wanted = wanted.transpose(1, 0, 2).reshape(share, -1)
    misfit_share = (output - wanted).astype(bf16)
    misfit_half = copies(misfit_share, "col_0").reshape(tok_rows, -1)
    other_half = swap(misfit_half, "col_1")
    misfit = jnp.concatenate(in_order(misfit_half, other_half, core), axis=0)

    def misfit_for(peer):
        return lax.dynamic_slice_in_dim(misfit, peer * rows, rows, 1).reshape(2, 1, tok_rows, rows)

    def into(result, piece, peer):
        return lax.dynamic_update_slice_in_dim(result, piece, peer, 1)

    out_pieces = [misfit_for(across)]
    for k in range(1, count_across):
        route = [(i, (i + k) % count_across) for i in range(count_across)]
        out_pieces.append(lax.ppermute(misfit_for((across + k) % count_across), "tok_1", route))

    scale_part = jnp.sum(misfit_share.astype(f32) * output, axis=0).reshape(count_across, -1, 128)
    extra = scale_part.shape[1]
    bins = bin_gradients(place, attended, misfit, plan, 1.0 / tokens)

    bins = jnp.broadcast_to(bins.reshape(1, -1, 128), (count_across, 2 * ENTRIES * GROUP // 128, 128))
    sums = jnp.concatenate([bins, scale_part], axis=1)
    sums = jnp.sum(exchange(sums, "tok_1"), axis=0)
    upper = sums.astype(bf16)
    lower = (sums[-extra:] - upper[-extra:].astype(f32)).astype(bf16)
    sums = copies(jnp.concatenate([upper, lower]), COL + ("tok_0",)).astype(f32)
    scale_sums = lax.dynamic_index_in_dim(sums.reshape(count_col, 2, -1, 128), high, 1, keepdims=False)
    scale_sums = jnp.sum(scale_sums[:, -2 * extra :], axis=0)
    scale_sums = (scale_sums[:extra] + scale_sums[extra:]).reshape(rows)
    bins = jnp.sum(sums[:, : -2 * extra], axis=0).astype(bf16)
    out_pieces, bins = lax.optimization_barrier((out_pieces, bins))
    misfit_out = jnp.zeros((2, count_across, tok_rows, rows), bf16)
    for k in range(count_across):
        misfit_out = into(misfit_out, out_pieces[k], (across + count_across - k) % count_across)
    bins = jnp.sum(copies(bins, "row").astype(f32), axis=0)
    return misfit_out.reshape(tokens, rows), scale_sums / (scales * tokens), bins.reshape(2, ENTRIES, GROUP)


def solution(mesh):
    split = Mesh(
        mesh.devices.reshape(4, 2, mesh.shape["row"], 2, 4),
        ("col_0", "col_1", "row", "tok_0", "tok_1"),
    )
    return jax.shard_map(
        device_part,
        mesh=split,
        in_specs=(
            P(TOK, COL_ROW),
            P(TOK, COL_ROW),
            P(TOK, COL_ROW),
            P(ROW_TOK, COL),
            P(ROW_TOK, COL),
            P(),
            P(),
            P(ROW_TOK),
            P(None, ROW_TOK),
        ),
        out_specs=(P(None, ROW_TOK), P(ROW_TOK), P()),
        check_vma=False,
    )
```

```python
import math

import jax
import jax.numpy as jnp
from jax import lax
from jax.experimental import pallas as pl
from jax.experimental.pallas import tpu as pltpu
from jax.sharding import Mesh
from jax.sharding import PartitionSpec as P


HEAD_DIM = 128
ENTRIES = 256
GROUP = 8
LOW = 8
HIGH = ENTRIES // LOW
TOK = ("tok_0", "tok_1")
ROW_TOK = ("row", "tok_0", "tok_1")
COL = ("col_0", "col_1")
COL_ROW = ("col_0", "col_1", "row")
f32, bf16 = jnp.float32, jnp.bfloat16


def exchange(pieces, axis):
    return lax.all_to_all(pieces, axis, 0, 0, tiled=True)


def copies(array, axis):
    pieces = jnp.broadcast_to(array[None], (lax.axis_size(axis), *array.shape))
    return exchange(pieces, axis)


def in_two(array, axis):
    upper = array.astype(bf16)
    return jnp.concatenate([upper, (array - upper.astype(f32)).astype(bf16)], axis=axis)


def swap(array, axis):
    return lax.ppermute(array, axis, [(0, 1), (1, 0)])


def in_order(mine, theirs, place):
    first = place == 0
    return jnp.where(first, mine, theirs), jnp.where(first, theirs, mine)


def dequant_kernel(block_ref, first_ref, second_ref, *refs):
    weight_ref, plan_ref, digit_ref = refs[-3:]
    groups, rows = weight_ref.shape[0] // GROUP, weight_ref.shape[1]
    tables, by_digit = [], []
    lanes = lax.broadcasted_iota(jnp.int32, (GROUP, 128), 1)
    for book_ref in (first_ref, second_ref):
        halves = [book_ref[:, start : start + 128].astype(f32) for start in (0, 128)]
        tables += halves
        digit_rows = []
        for d in range(LOW):
            place = (lanes * LOW + d) & 127
            near, far = (
                jnp.take_along_axis(half, place, axis=1, mode="promise_in_bounds") for half in halves
            )
            digit_rows.append(jnp.where(lanes < 128 // LOW, near, far))
        by_digit.append(jnp.concatenate(digit_rows, axis=0)[:, :HIGH].astype(bf16))
    plan_ref[...] = block_ref[...]
    scale = jnp.broadcast_to(block_ref[groups : groups + 1, :], (GROUP, rows))
    packed = block_ref[:groups, :].astype(jnp.int32)
    for book in range(2):
        code = (packed & 255) if book == 0 else (packed >> 8)
        digit_ref[2 * book] = (code & (LOW - 1)).astype(f32)
        digit_ref[2 * book + 1] = (code >> 3).astype(f32)
    at = lax.broadcasted_iota(jnp.int32, (16, rows), 0)
    high_rows = [(16 * d + at).astype(f32).astype(bf16) for d in range(HIGH // 16)]
    zero, one = jnp.zeros((16, rows), bf16), jnp.ones((16, rows), bf16)

    def picked(book, half, place):
        return jnp.take_along_axis(tables[2 * book + half], place, axis=1, mode="promise_in_bounds")

    def by_gather(g):
        both = jnp.broadcast_to(block_ref[pl.ds(g, 1), :], (GROUP, rows)).astype(jnp.int32)
        parts = []
        for start in range(0, rows, 128):
            packed = both[:, start : start + 128]
            total = None
            for book in range(2):
                code = (packed & 255) if book == 0 else (packed >> 8)
                place = code & 127
                entry = jnp.where(code >= 128, picked(book, 1, place), picked(book, 0, place))
                total = entry if total is None else total + entry
            parts.append(total * scale[:, start : start + 128])
        return jnp.concatenate(parts, axis=1)

    def by_product(g):
        total = None
        for book in range(2):
            high = jnp.broadcast_to(digit_ref[2 * book + 1, pl.ds(g, 1), :], (16, rows)).astype(bf16)
            hot = jnp.concatenate([jnp.where(high == r, one, zero) for r in high_rows], axis=0)
            near = jnp.dot(by_digit[book], hot, preferred_element_type=f32)
            low = jnp.broadcast_to(digit_ref[2 * book, pl.ds(g, 1), :], (GROUP, rows))
            entry = near[:GROUP]
            for d in range(1, LOW):
                entry = jnp.where(low == float(d), near[d * GROUP : (d + 1) * GROUP], entry)
            total = entry if total is None else total + entry
        return total * scale

    chunk = 16

    def step(i, carry):
        for k in range(0, chunk, 2):
            g = i * chunk + k
            pair = jnp.concatenate([by_gather(g), by_product(g + 1)], axis=0)
            weight_ref[pl.ds(pl.multiple_of(g * GROUP, 16), 16), :] = pair.astype(bf16)
        return carry

    lax.fori_loop(0, groups // chunk, step, 0, unroll=2)


def dequantize(block, books, at, blocks, groups, before=()):
    rows = block.shape[1]
    return pl.pallas_call(
        dequant_kernel,
        grid=(1,),
        in_specs=[
            pl.BlockSpec(block.shape, lambda i: (0, 0)),
            pl.BlockSpec(books[0].shape, lambda i: (0, 0)),
            pl.BlockSpec(books[1].shape, lambda i: (0, 0)),
        ]
        + [pl.BlockSpec(memory_space=pl.ANY)] * len(before),
        out_specs=[
            pl.BlockSpec((None, groups * GROUP, rows), lambda i: (at, 0, 0)),
            pl.BlockSpec((None, *block.shape), lambda i: (at, 0, 0)),
        ],
        out_shape=[
            jax.ShapeDtypeStruct((blocks, groups * GROUP, rows), bf16),
            jax.ShapeDtypeStruct((blocks, *block.shape), f32),
        ],
        scratch_shapes=[pltpu.VMEM((4, groups, rows), f32)],
        input_output_aliases={3: 0, 4: 1} if before else {},
        cost_estimate=pl.CostEstimate(
            flops=8_000_000_000, transcendentals=0, bytes_accessed=1_500_000
        ),
        name="dequant",
    )(block, *books, *before)


def project_kernel(core_ref, att_ref, weight_ref, keep_ref, send_ref, all_ref):
    steps, tokens, width = att_ref.shape
    half = tokens // 2
    total = None
    for z in range(steps):
        part = jnp.dot(
            att_ref[z], weight_ref[z * width : (z + 1) * width, :], preferred_element_type=f32
        )
        total = part if total is None else total + part
    all_ref[...] = total
    keep_ref[...] = all_ref[pl.ds(pl.multiple_of(core_ref[0] * half, half), half), :]
    send_ref[...] = all_ref[pl.ds(pl.multiple_of((1 - core_ref[0]) * half, half), half), :]


def project(core, attended, weight):
    steps, tokens, width = attended.shape
    blocks, depth, rows = weight.shape
    out = jax.ShapeDtypeStruct((tokens // 2, blocks * rows), f32)
    out_spec = pl.BlockSpec((tokens // 2, rows), lambda i, core: (0, i))
    return pl.pallas_call(
        project_kernel,
        grid_spec=pltpu.PrefetchScalarGridSpec(
            num_scalar_prefetch=1,
            grid=(blocks,),
            in_specs=[
                pl.BlockSpec((steps, tokens, width), lambda i, core: (0, 0, 0)),
                pl.BlockSpec((None, depth, rows), lambda i, core: (i, 0, 0)),
            ],
            out_specs=[out_spec, out_spec],
            scratch_shapes=[pltpu.VMEM((tokens, rows), f32)],
        ),
        out_shape=[out, out],
        name="project",
    )(core, attended, weight)


def bins_kernel(scaling, att_ref, misfit_ref, plan_ref, bins_ref, grad_ref, digit_ref):
    groups, rows = digit_ref.shape[1:]
    steps, _, width = att_ref.shape
    scale = plan_ref[groups : groups + 1, :] * scaling
    misfit = misfit_ref[...]
    for z in range(steps):
        weight_grad = lax.dot_general(
            att_ref[z], misfit, (((0,), (0,)), ((), ())), preferred_element_type=f32
        )
        grad_ref[z * width : (z + 1) * width, :] = weight_grad * scale
    packed = plan_ref[:groups, :].astype(jnp.int32)
    for book in range(2):
        code = (packed & 255) if book == 0 else (packed >> 8)
        digit_ref[2 * book] = (code & (LOW - 1)).astype(f32)
        digit_ref[2 * book + 1] = (code >> 3).astype(f32)
    at = lax.broadcasted_iota(jnp.int32, (16, rows), 0)
    low_rows = [(2 * d + (at >= 8).astype(jnp.int32)).astype(f32).astype(bf16) for d in range(LOW // 2)]
    high_rows = [(16 * d + at).astype(f32).astype(bf16) for d in range(HIGH // 16)]
    zero, one = jnp.zeros((16, rows), bf16), jnp.ones((16, rows), bf16)
    chunk = 8

    def digit(which, g):
        return jnp.broadcast_to(digit_ref[which, pl.ds(g, 1), :], (16, rows)).astype(bf16)

    def step(i, totals):
        twice = []
        for k in range(chunk):
            entry = grad_ref[pl.ds(pl.multiple_of((i * chunk + k) * GROUP, GROUP), GROUP), :]
            twice.append(jnp.concatenate([entry, entry], axis=0).astype(bf16))
        done = []
        for book in range(2):
            highs, lows = [], []
            for k in range(chunk):
                low, high = digit(2 * book, i * chunk + k), digit(2 * book + 1, i * chunk + k)
                lows.append(
                    jnp.concatenate([jnp.where(low == r, twice[k], zero) for r in low_rows], axis=0)
                )
                highs.append(
                    jnp.concatenate([jnp.where(high == r, one, zero) for r in high_rows], axis=0)
                )
            part = lax.dot_general(
                jnp.concatenate(highs, axis=1),
                jnp.concatenate(lows, axis=1),
                (((1,), (1,)), ((), ())),
                preferred_element_type=f32,
            )
            done.append(totals[book] + part)
        return tuple(done)

    empty = jnp.zeros((HIGH, LOW * GROUP), f32)
    totals = lax.fori_loop(0, groups // chunk, step, (empty, empty), unroll=2)

    @pl.when(pl.program_id(0) == 0)
    def _():
        bins_ref[...] = jnp.zeros_like(bins_ref)

    for book in range(2):
        bins_ref[book] += totals[book]


def bin_gradients(attended, misfit, plan, groups, scaling):
    steps, tokens, width = attended.shape
    blocks, depth, rows = plan.shape
    return pl.pallas_call(
        lambda *refs: bins_kernel(scaling, *refs),
        grid=(blocks,),
        in_specs=[
            pl.BlockSpec((steps, tokens, width), lambda i: (0, 0, 0)),
            pl.BlockSpec((tokens, rows), lambda i: (0, i)),
            pl.BlockSpec((None, depth, rows), lambda i: (i, 0, 0)),
        ],
        out_specs=pl.BlockSpec((2, HIGH, LOW * GROUP), lambda i: (0, 0, 0)),
        out_shape=jax.ShapeDtypeStruct((2, HIGH, LOW * GROUP), f32),
        scratch_shapes=[
            pltpu.VMEM((steps * width, rows), f32),
            pltpu.VMEM((4, groups, rows), f32),
        ],
        cost_estimate=pl.CostEstimate(
            flops=blocks * 8_000_000_000, transcendentals=0, bytes_accessed=blocks * 2_000_000
        ),
        name="bins",
    )(attended, misfit, plan)


def attend(queries, keys, values, query_places, key_places):
    scores = jnp.einsum("qd,kd->qk", queries, keys, preferred_element_type=f32) / math.sqrt(HEAD_DIM)
    allowed = key_places[None, :] <= query_places[:, None]
    row_max = jnp.max(jnp.where(allowed, scores, -1e30), axis=-1, keepdims=True)
    exponent = jnp.where(allowed, jnp.exp(scores - row_max), 0.0)
    row_sum = jnp.sum(exponent, axis=-1, keepdims=True)
    weighted = jnp.einsum("qk,kd->qd", exponent.astype(bf16), values, preferred_element_type=f32)
    return (weighted / row_sum).astype(bf16)


def device_part(
    queries, key_rows, values, code_first, code_second, book_first, book_second, scales, target
):
    tok_rows, _ = queries.shape
    high, across = lax.axis_index("tok_0"), lax.axis_index("tok_1")
    count_across = lax.axis_size("tok_1")
    lane, core = lax.axis_index("col_0"), lax.axis_index("col_1")
    count_lane, count_col = lax.axis_size("col_0"), lax.axis_size(COL)
    rows = code_first.shape[0]
    tokens = lax.axis_size(TOK) * tok_rows

    def of_head(head):
        picked = [
            lax.dynamic_slice_in_dim(array, head * HEAD_DIM, HEAD_DIM, 1)
            for array in (queries, key_rows, values)
        ]
        return jnp.concatenate(picked, axis=1)

    mine = of_head(high)
    both = jnp.concatenate(in_order(mine, swap(of_head(1 - high), "tok_0"), high))
    pairs = copies(both[:, HEAD_DIM:], "tok_1")
    block = lax.iota(jnp.int32, 2)[:, None] * (count_across * tok_rows)
    block = block + lax.iota(jnp.int32, tok_rows)[None, :]
    query_places = (block + across * tok_rows).reshape(-1)
    key_places = lax.iota(jnp.int32, count_across)[:, None, None] * tok_rows + block[None]
    pairs = pairs.reshape(tokens, 2 * HEAD_DIM)
    head_out = attend(
        both[:, :HEAD_DIM], pairs[:, :HEAD_DIM], pairs[:, HEAD_DIM:], query_places, key_places.reshape(-1)
    )
    other_out = swap(head_out, "tok_0")
    attended = copies(jnp.concatenate(in_order(head_out, other_out, high), axis=1), "row")

    own_codes = (code_first + ENTRIES * code_second).T.astype(f32)
    groups = own_codes.shape[0]
    share = tok_rows // count_lane
    wanted = target.reshape(2, count_across, count_lane, share, rows)
    wanted = lax.dynamic_index_in_dim(wanted, core, 0, keepdims=False)
    wanted = lax.dynamic_index_in_dim(wanted, lane, 1, keepdims=False).astype(f32)
    own_scales = jnp.broadcast_to(scales[None], (8, rows))

    def block_for(peer):
        part = lax.dynamic_index_in_dim(wanted, peer, 0, keepdims=False)
        return jnp.concatenate([own_codes, own_scales, part], axis=0)

    own_block = block_for(across)
    books = (book_first.T, book_second.T)
    received = [own_block]
    built = dequantize(own_block, books, 0, count_across, groups)
    for k in range(1, count_across):
        sent, _ = lax.optimization_barrier((block_for((across + count_across - k) % count_across), pairs))
        route = [((i + k) % count_across, i) for i in range(count_across)]
        received.append(lax.ppermute(sent, "tok_1", route))
        built = dequantize(received[k], books, k, count_across, groups, built)
    weight, plan = built

    keep, send = project(core[None], attended, weight)
    half_sum = (keep + swap(send, "col_1")).astype(bf16)
    parts = exchange(half_sum.reshape(count_lane, share, -1), "col_0")
    output = jnp.sum(parts.astype(f32), axis=0)
    misfit_share = (output - plan[:, groups + 8 :].transpose(1, 0, 2).reshape(share, -1)).astype(bf16)
    misfit_half = copies(misfit_share, "col_0").reshape(tok_rows, -1)
    other_half = swap(misfit_half, "col_1")
    misfit = jnp.concatenate(in_order(misfit_half, other_half, core), axis=0)

    out_pieces = []
    for k in range(count_across):
        piece = misfit[:, k * rows : (k + 1) * rows].reshape(2, 1, tok_rows, rows)
        route = [(i, (i + k) % count_across) for i in range(count_across)]
        out_pieces.append(lax.ppermute(piece, "tok_1", route) if k else piece)

    scale_part = jnp.sum(misfit_share.astype(f32) * output, axis=0).reshape(count_across, -1, 128)
    extra = scale_part.shape[1]
    scale_part = jnp.concatenate([scale_part, scale_part], axis=0)
    start = (count_across - across) % count_across
    scale_part = in_two(lax.dynamic_slice_in_dim(scale_part, start, count_across, 0), 1)
    bins = bin_gradients(attended, misfit, plan, groups, 1.0 / tokens)

    count_row = lax.axis_size("row")
    bins = bins.reshape(-1, 128).astype(bf16)
    bins = jnp.broadcast_to(bins[None, None], (count_row, count_across, *bins.shape))
    scale_part = jnp.broadcast_to(scale_part[None], (count_row, *scale_part.shape))
    sums = jnp.concatenate([bins, scale_part], axis=2).reshape(count_row * count_across, -1, 128)
    sums = exchange(sums, ("row", "tok_1"))
    own_row = sums.reshape(count_row, count_across, -1, 128)[:, :, -2 * extra :]
    own_row = lax.dynamic_index_in_dim(own_row, lax.axis_index("row"), 0, keepdims=False)
    own_row = jnp.sum(own_row.astype(f32), axis=0)
    scale_part = in_two(own_row[:extra] + own_row[extra:], 0)
    bins = jnp.sum(sums[:, : -2 * extra].astype(f32), axis=0).astype(bf16)
    sums = copies(jnp.concatenate([bins, scale_part]), COL + ("tok_0",))
    scale_part = sums.reshape(count_col, 2, -1, 128)[:, :, -2 * extra :]
    scale_part = lax.dynamic_index_in_dim(scale_part, high, 1, keepdims=False)
    scale_part = jnp.sum(scale_part.astype(f32), axis=0)
    grad_scales = (scale_part[:extra] + scale_part[extra:]).reshape(rows) / (scales * tokens)
    grad_books = jnp.sum(sums[:, : -2 * extra].astype(f32), axis=0).reshape(2, ENTRIES, GROUP)

    misfit_out = jnp.zeros((2, count_across, tok_rows, rows), bf16)
    for k in range(count_across):
        peer = (across + count_across - k) % count_across
        misfit_out = lax.dynamic_update_slice_in_dim(misfit_out, out_pieces[k], peer, 1)
    return misfit_out.reshape(tokens, rows), grad_scales, grad_books


def solution(mesh):
    split = Mesh(
        mesh.devices.reshape(4, 2, mesh.shape["row"], 2, 4),
        ("col_0", "col_1", "row", "tok_0", "tok_1"),
    )
    return jax.shard_map(
        device_part,
        mesh=split,
        in_specs=(
            P(TOK, COL_ROW),
            P(TOK, COL_ROW),
            P(TOK, COL_ROW),
            P(ROW_TOK, COL),
            P(ROW_TOK, COL),
            P(),
            P(),
            P(ROW_TOK),
            P(None, ROW_TOK),
        ),
        out_specs=(P(None, ROW_TOK), P(ROW_TOK), P()),
        check_vma=False,
    )
```

```python
import math

import jax
import jax.numpy as jnp
from jax import lax
from jax.experimental import pallas as pl
from jax.experimental.pallas import tpu as pltpu
from jax.sharding import Mesh
from jax.sharding import PartitionSpec as P


HEAD_DIM = 128
ENTRIES = 256
GROUP = 8
LOW = 8
HIGH = ENTRIES // LOW
TOK = ("tok_0", "tok_1")
ROW_TOK = ("row", "tok_0", "tok_1")
COL = ("col_0", "col_1")
COL_ROW = ("col_0", "col_1", "row")
f32, bf16 = jnp.float32, jnp.bfloat16


def exchange(pieces, axis):
    return lax.all_to_all(pieces, axis, 0, 0, tiled=True)


def copies(array, axis):
    pieces = jnp.broadcast_to(array[None], (lax.axis_size(axis), *array.shape))
    return exchange(pieces, axis)


def in_two(array, axis):
    upper = array.astype(bf16)
    return jnp.concatenate([upper, (array - upper.astype(f32)).astype(bf16)], axis=axis)


def swap(array, axis):
    return lax.ppermute(array, axis, [(0, 1), (1, 0)])


def in_order(mine, theirs, place):
    first = place == 0
    return jnp.where(first, mine, theirs), jnp.where(first, theirs, mine)


def dequant_kernel(block_ref, first_ref, second_ref, *refs):
    weight_ref, plan_ref, digit_ref = refs[-3:]
    groups, rows = weight_ref.shape[0] // GROUP, weight_ref.shape[1]
    tables, by_digit = [], []
    lanes = lax.broadcasted_iota(jnp.int32, (GROUP, 128), 1)
    for book_ref in (first_ref, second_ref):
        halves = [book_ref[:, start : start + 128].astype(f32) for start in (0, 128)]
        tables += halves
        digit_rows = []
        for d in range(LOW):
            place = (lanes * LOW + d) & 127
            near, far = (
                jnp.take_along_axis(half, place, axis=1, mode="promise_in_bounds") for half in halves
            )
            digit_rows.append(jnp.where(lanes < 128 // LOW, near, far))
        by_digit.append(jnp.concatenate(digit_rows, axis=0)[:, :HIGH].astype(bf16))
    plan_ref[...] = block_ref[...]
    scale = jnp.broadcast_to(block_ref[groups : groups + 1, :], (GROUP, rows))
    packed = block_ref[:groups, :].astype(jnp.int32)
    for book in range(2):
        code = (packed & 255) if book == 0 else (packed >> 8)
        digit_ref[2 * book] = (code & (LOW - 1)).astype(f32)
        digit_ref[2 * book + 1] = (code >> 3).astype(f32)
    at = lax.broadcasted_iota(jnp.int32, (16, rows), 0)
    high_rows = [(16 * d + at).astype(f32).astype(bf16) for d in range(HIGH // 16)]
    zero, one = jnp.zeros((16, rows), bf16), jnp.ones((16, rows), bf16)

    def picked(book, half, place):
        return jnp.take_along_axis(tables[2 * book + half], place, axis=1, mode="promise_in_bounds")

    def by_gather(g):
        both = jnp.broadcast_to(block_ref[pl.ds(g, 1), :], (GROUP, rows)).astype(jnp.int32)
        parts = []
        for start in range(0, rows, 128):
            packed = both[:, start : start + 128]
            total = None
            for book in range(2):
                code = (packed & 255) if book == 0 else (packed >> 8)
                place = code & 127
                entry = jnp.where(code >= 128, picked(book, 1, place), picked(book, 0, place))
                total = entry if total is None else total + entry
            parts.append(total * scale[:, start : start + 128])
        return jnp.concatenate(parts, axis=1)

    def by_product(g):
        total = None
        for book in range(2):
            high = jnp.broadcast_to(digit_ref[2 * book + 1, pl.ds(g, 1), :], (16, rows)).astype(bf16)
            hot = jnp.concatenate([jnp.where(high == r, one, zero) for r in high_rows], axis=0)
            near = jnp.dot(by_digit[book], hot, preferred_element_type=f32)
            low = jnp.broadcast_to(digit_ref[2 * book, pl.ds(g, 1), :], (GROUP, rows))
            entry = near[:GROUP]
            for d in range(1, LOW):
                entry = jnp.where(low == float(d), near[d * GROUP : (d + 1) * GROUP], entry)
            total = entry if total is None else total + entry
        return total * scale

    chunk = 16

    def step(i, carry):
        for k in range(0, chunk, 2):
            g = i * chunk + k
            pair = jnp.concatenate([by_gather(g), by_product(g + 1)], axis=0)
            weight_ref[pl.ds(pl.multiple_of(g * GROUP, 16), 16), :] = pair.astype(bf16)
        return carry

    lax.fori_loop(0, groups // chunk, step, 0, unroll=2)


def dequantize(block, books, at, blocks, groups, before=()):
    rows = block.shape[1]
    return pl.pallas_call(
        dequant_kernel,
        grid=(1,),
        in_specs=[
            pl.BlockSpec(memory_space=pltpu.VMEM),
            pl.BlockSpec(books[0].shape, lambda i: (0, 0)),
            pl.BlockSpec(books[1].shape, lambda i: (0, 0)),
        ]
        + [pl.BlockSpec(memory_space=pl.ANY)] * len(before),
        out_specs=[
            pl.BlockSpec((None, groups * GROUP, rows), lambda i: (at, 0, 0)),
            pl.BlockSpec((None, *block.shape), lambda i: (at, 0, 0)),
        ],
        out_shape=[
            jax.ShapeDtypeStruct((blocks, groups * GROUP, rows), bf16),
            jax.ShapeDtypeStruct((blocks, *block.shape), f32),
        ],
        scratch_shapes=[pltpu.VMEM((4, groups, rows), f32)],
        input_output_aliases={3: 0, 4: 1} if before else {},
        cost_estimate=pl.CostEstimate(
            flops=8_000_000_000, transcendentals=0, bytes_accessed=1_500_000
        ),
        name="dequant",
    )(block, *books, *before)


def project_kernel(core_ref, att_ref, weight_ref, keep_ref, send_ref, all_ref):
    steps, tokens, width = att_ref.shape
    half = tokens // 2
    total = None
    for z in range(steps):
        part = jnp.dot(
            att_ref[z], weight_ref[z * width : (z + 1) * width, :], preferred_element_type=f32
        )
        total = part if total is None else total + part
    all_ref[...] = total
    keep_ref[...] = all_ref[pl.ds(pl.multiple_of(core_ref[0] * half, half), half), :]
    send_ref[...] = all_ref[pl.ds(pl.multiple_of((1 - core_ref[0]) * half, half), half), :]


def project(core, attended, weight):
    _, tokens, _ = attended.shape
    blocks, depth, rows = weight.shape
    out = jax.ShapeDtypeStruct((tokens // 2, blocks * rows), f32)
    out_spec = pl.BlockSpec((tokens // 2, rows), lambda i, core: (0, i))
    return pl.pallas_call(
        project_kernel,
        grid_spec=pltpu.PrefetchScalarGridSpec(
            num_scalar_prefetch=1,
            grid=(blocks,),
            in_specs=[
                pl.BlockSpec(memory_space=pltpu.VMEM),
                pl.BlockSpec((None, depth, rows), lambda i, core: (i, 0, 0)),
            ],
            out_specs=[out_spec, out_spec],
            scratch_shapes=[pltpu.VMEM((tokens, rows), f32)],
        ),
        out_shape=[out, out],
        name="project",
    )(core, attended, weight)


def bins_kernel(scaling, *refs):
    own_att_ref, their_att_ref, own_misfit_ref, their_misfit_ref = refs[:4]
    plan_ref, bins_ref, grad_ref, digit_ref = refs[4:]
    groups, rows = digit_ref.shape[1:]
    steps, _, width = own_att_ref.shape
    scale = plan_ref[groups : groups + 1, :] * scaling
    for z in range(steps):
        weight_grad = None
        for att_ref, misfit_ref in ((own_att_ref, own_misfit_ref), (their_att_ref, their_misfit_ref)):
            part = lax.dot_general(
                att_ref[z], misfit_ref[...], (((0,), (0,)), ((), ())), preferred_element_type=f32
            )
            weight_grad = part if weight_grad is None else weight_grad + part
        grad_ref[z * width : (z + 1) * width, :] = weight_grad * scale
    packed = plan_ref[:groups, :].astype(jnp.int32)
    for book in range(2):
        code = (packed & 255) if book == 0 else (packed >> 8)
        digit_ref[2 * book] = (code & (LOW - 1)).astype(f32)
        digit_ref[2 * book + 1] = (code >> 3).astype(f32)
    at = lax.broadcasted_iota(jnp.int32, (16, rows), 0)
    low_rows = [(2 * d + (at >= 8).astype(jnp.int32)).astype(f32).astype(bf16) for d in range(LOW // 2)]
    high_rows = [(16 * d + at).astype(f32).astype(bf16) for d in range(HIGH // 16)]
    zero, one = jnp.zeros((16, rows), bf16), jnp.ones((16, rows), bf16)
    chunk = 8

    def digit(which, g):
        return jnp.broadcast_to(digit_ref[which, pl.ds(g, 1), :], (16, rows)).astype(bf16)

    def step(i, totals):
        twice = []
        for k in range(chunk):
            entry = grad_ref[pl.ds(pl.multiple_of((i * chunk + k) * GROUP, GROUP), GROUP), :]
            twice.append(jnp.concatenate([entry, entry], axis=0).astype(bf16))
        done = []
        for book in range(2):
            highs, lows = [], []
            for k in range(chunk):
                low, high = digit(2 * book, i * chunk + k), digit(2 * book + 1, i * chunk + k)
                lows.append(
                    jnp.concatenate([jnp.where(low == r, twice[k], zero) for r in low_rows], axis=0)
                )
                highs.append(
                    jnp.concatenate([jnp.where(high == r, one, zero) for r in high_rows], axis=0)
                )
            part = lax.dot_general(
                jnp.concatenate(highs, axis=1),
                jnp.concatenate(lows, axis=1),
                (((1,), (1,)), ((), ())),
                preferred_element_type=f32,
            )
            done.append(totals[book] + part)
        return tuple(done)

    empty = jnp.zeros((HIGH, LOW * GROUP), f32)
    totals = lax.fori_loop(0, groups // chunk, step, (empty, empty), unroll=2)

    @pl.when(pl.program_id(0) == 0)
    def _():
        bins_ref[...] = jnp.zeros_like(bins_ref)

    for book in range(2):
        bins_ref[book] += totals[book]


def bin_gradients(own, theirs, plan, groups, scaling):
    steps, tokens, width = own[0].shape
    blocks, depth, rows = plan.shape
    whole = pl.BlockSpec(memory_space=pltpu.VMEM)
    return pl.pallas_call(
        lambda *refs: bins_kernel(scaling, *refs),
        grid=(blocks // 2,),
        in_specs=[
            whole,
            whole,
            pl.BlockSpec((tokens, rows), lambda i: (0, 2 * i)),
            pl.BlockSpec((tokens, rows), lambda i: (0, i)),
            pl.BlockSpec((None, depth, rows), lambda i: (2 * i, 0, 0)),
        ],
        out_specs=pl.BlockSpec((2, HIGH, LOW * GROUP), lambda i: (0, 0, 0)),
        out_shape=jax.ShapeDtypeStruct((2, HIGH, LOW * GROUP), f32),
        scratch_shapes=[
            pltpu.VMEM((steps * width, rows), f32),
            pltpu.VMEM((4, groups, rows), f32),
        ],
        cost_estimate=pl.CostEstimate(
            flops=blocks * 4_000_000_000, transcendentals=0, bytes_accessed=blocks * 1_000_000
        ),
        name="bins",
    )(own[0], theirs[0], own[1], theirs[1], plan)


def attend(queries, keys, values, query_places, key_places):
    scores = jnp.einsum("qd,kd->qk", queries, keys, preferred_element_type=f32) / math.sqrt(HEAD_DIM)
    allowed = key_places[None, :] <= query_places[:, None]
    row_max = jnp.max(jnp.where(allowed, scores, -1e30), axis=-1, keepdims=True)
    exponent = jnp.where(allowed, jnp.exp(scores - row_max), 0.0)
    row_sum = jnp.sum(exponent, axis=-1, keepdims=True)
    weighted = jnp.einsum("qk,kd->qd", exponent.astype(bf16), values, preferred_element_type=f32)
    return (weighted / row_sum).astype(bf16)


def device_part(
    queries, key_rows, values, code_first, code_second, book_first, book_second, scales, target
):
    tok_rows, _ = queries.shape
    high, across = lax.axis_index("tok_0"), lax.axis_index("tok_1")
    count_across = lax.axis_size("tok_1")
    lane, core = lax.axis_index("col_0"), lax.axis_index("col_1")
    count_lane, count_col = lax.axis_size("col_0"), lax.axis_size(COL)
    rows = code_first.shape[0]
    tokens = lax.axis_size(TOK) * tok_rows

    def of_head(head):
        picked = [
            lax.dynamic_slice_in_dim(array, head * HEAD_DIM, HEAD_DIM, 1)
            for array in (queries, key_rows, values)
        ]
        return jnp.concatenate(picked, axis=1)

    mine = of_head(high)
    both = jnp.concatenate(in_order(mine, swap(of_head(1 - high), "tok_0"), high))
    pairs = copies(both[:, HEAD_DIM:], "tok_1")
    block = lax.iota(jnp.int32, 2)[:, None] * (count_across * tok_rows)
    block = block + lax.iota(jnp.int32, tok_rows)[None, :]
    query_places = (block + across * tok_rows).reshape(-1)
    key_places = lax.iota(jnp.int32, count_across)[:, None, None] * tok_rows + block[None]
    pairs = pairs.reshape(tokens, 2 * HEAD_DIM)
    head_out = attend(
        both[:, :HEAD_DIM], pairs[:, :HEAD_DIM], pairs[:, HEAD_DIM:], query_places, key_places.reshape(-1)
    )
    other_out = swap(head_out, "tok_0")
    attended = copies(jnp.concatenate(in_order(head_out, other_out, high), axis=1), "row")

    own_codes = (code_first + ENTRIES * code_second).T.astype(f32)
    groups = own_codes.shape[0]
    share = tok_rows // count_lane
    wanted = target.reshape(2, count_across, count_lane, share, rows)
    wanted = lax.dynamic_index_in_dim(wanted, core, 0, keepdims=False)
    wanted = lax.dynamic_index_in_dim(wanted, lane, 1, keepdims=False).astype(f32)
    own_scales = jnp.broadcast_to(scales[None], (8, rows))

    def block_for(peer):
        part = lax.dynamic_index_in_dim(wanted, peer, 0, keepdims=False)
        return jnp.concatenate([own_codes, own_scales, part], axis=0)

    own_block = block_for(across)
    books = (book_first.T, book_second.T)
    received = [own_block]
    built = dequantize(own_block, books, 0, count_across, groups)
    for k in range(1, count_across):
        sent, _ = lax.optimization_barrier((block_for((across + count_across - k) % count_across), pairs))
        route = [((i + k) % count_across, i) for i in range(count_across)]
        received.append(lax.ppermute(sent, "tok_1", route))
        built = dequantize(received[k], books, k, count_across, groups, built)
    weight, plan = built

    keep, send = project(core[None], attended, weight)
    pair = [(0, 1), (1, 0), (2, 3), (3, 2)]
    their_attended = lax.ppermute(attended, "tok_1", pair)
    half_sum = (keep + swap(send, "col_1")).astype(bf16)
    parts = exchange(half_sum.reshape(count_lane, share, -1), "col_0")
    output = jnp.sum(parts.astype(f32), axis=0)
    misfit_share = (output - plan[:, groups + 8 :].transpose(1, 0, 2).reshape(share, -1)).astype(bf16)
    misfit_half = copies(misfit_share, "col_0").reshape(tok_rows, -1)
    other_half = swap(misfit_half, "col_1")
    misfit = jnp.concatenate(in_order(misfit_half, other_half, core), axis=0)

    even = across % 2 == 0
    blocks = [misfit[:, k * rows : (k + 1) * rows] for k in range(count_across)]
    pairs_own, pairs_next = jnp.where(even, blocks[1], blocks[3]), jnp.where(even, blocks[3], blocks[1])
    their_misfit = lax.ppermute(jnp.concatenate([pairs_own, pairs_next], axis=1), "tok_1", pair)
    from_across = lax.ppermute(blocks[2], "tok_1", [(0, 2), (1, 3), (2, 0), (3, 1)])
    from_beside = lax.ppermute(pairs_next, "tok_1", [(1, 2), (2, 1), (3, 0), (0, 3)])
    step = jnp.where(even, 1, count_across - 1)
    out_pieces = (
        (blocks[0], across),
        (their_misfit[:, :rows], (across + step) % count_across),
        (from_across, (across + 2) % count_across),
        (from_beside, (across + count_across - step) % count_across),
    )

    scale_part = jnp.sum(misfit_share.astype(f32) * output, axis=0).reshape(count_across, -1, 128)
    extra = scale_part.shape[1]
    scale_part = jnp.concatenate([scale_part, scale_part], axis=0)
    start = (count_across - across) % count_across
    scale_part = in_two(lax.dynamic_slice_in_dim(scale_part, start, count_across, 0), 1)
    theirs = (their_attended, their_misfit)
    bins = bin_gradients((attended, misfit), theirs, plan, groups, 1.0 / tokens)

    count_row = lax.axis_size("row")
    bins = bins.reshape(-1, 128).astype(bf16)
    bins = jnp.broadcast_to(bins[None, None], (count_row, count_across, *bins.shape))
    scale_part = jnp.broadcast_to(scale_part[None], (count_row, *scale_part.shape))
    sums = jnp.concatenate([bins, scale_part], axis=2).reshape(count_row * count_across, -1, 128)
    sums = exchange(sums, ("row", "tok_1"))
    own_row = sums.reshape(count_row, count_across, -1, 128)[:, :, -2 * extra :]
    own_row = lax.dynamic_index_in_dim(own_row, lax.axis_index("row"), 0, keepdims=False)
    own_row = jnp.sum(own_row.astype(f32), axis=0)
    scale_part = in_two(own_row[:extra] + own_row[extra:], 0)
    bins = jnp.sum(sums[:, : -2 * extra].astype(f32), axis=0).astype(bf16)
    sums = copies(jnp.concatenate([bins, scale_part]), COL + ("tok_0",))
    scale_part = sums.reshape(count_col, 2, -1, 128)[:, :, -2 * extra :]
    scale_part = lax.dynamic_index_in_dim(scale_part, high, 1, keepdims=False)
    scale_part = jnp.sum(scale_part.astype(f32), axis=0)
    grad_scales = (scale_part[:extra] + scale_part[extra:]).reshape(rows) / (scales * tokens)
    grad_books = jnp.sum(sums[:, : -2 * extra].astype(f32), axis=0).reshape(2, ENTRIES, GROUP)

    misfit_out = jnp.zeros((2, count_across, tok_rows, rows), bf16)
    for piece, peer in out_pieces:
        piece = piece.reshape(2, 1, tok_rows, rows)
        misfit_out = lax.dynamic_update_slice_in_dim(misfit_out, piece, peer, 1)
    return misfit_out.reshape(tokens, rows), grad_scales, grad_books


def solution(mesh):
    split = Mesh(
        mesh.devices.reshape(4, 2, mesh.shape["row"], 2, 4),
        ("col_0", "col_1", "row", "tok_0", "tok_1"),
    )
    return jax.shard_map(
        device_part,
        mesh=split,
        in_specs=(
            P(TOK, COL_ROW),
            P(TOK, COL_ROW),
            P(TOK, COL_ROW),
            P(ROW_TOK, COL),
            P(ROW_TOK, COL),
            P(),
            P(),
            P(ROW_TOK),
            P(None, ROW_TOK),
        ),
        out_specs=(P(None, ROW_TOK), P(ROW_TOK), P()),
        check_vma=False,
    )
```

```python
import math

import jax
import jax.numpy as jnp
from jax import lax
from jax.experimental import pallas as pl
from jax.experimental.pallas import tpu as pltpu
from jax.sharding import Mesh
from jax.sharding import PartitionSpec as P


HEAD_DIM = 128
ENTRIES = 256
GROUP = 8
LOW = 8
HIGH = ENTRIES // LOW
TOK = ("tok_0", "tok_1")
ROW_TOK = ("row", "tok_0", "tok_1")
COL = ("col_0", "col_1")
COL_ROW = ("col_0", "col_1", "row")
f32, bf16 = jnp.float32, jnp.bfloat16


def exchange(pieces, axis):
    return lax.all_to_all(pieces, axis, 0, 0, tiled=True)


def copies(array, axis):
    pieces = jnp.broadcast_to(array[None], (lax.axis_size(axis), *array.shape))
    return exchange(pieces, axis)


def in_two(array, axis):
    upper = array.astype(bf16)
    return jnp.concatenate([upper, (array - upper.astype(f32)).astype(bf16)], axis=axis)


def swap(array, axis):
    return lax.ppermute(array, axis, [(0, 1), (1, 0)])


def in_order(mine, theirs, place):
    first = place == 0
    return jnp.where(first, mine, theirs), jnp.where(first, theirs, mine)


def dequant_kernel(block_ref, first_ref, second_ref, *refs):
    weight_ref, plan_ref, digit_ref = refs[-3:]
    groups, rows = weight_ref.shape[0] // GROUP, weight_ref.shape[1]
    tables, by_digit = [], []
    lanes = lax.broadcasted_iota(jnp.int32, (GROUP, 128), 1)
    for book_ref in (first_ref, second_ref):
        halves = [book_ref[:, start : start + 128].astype(f32) for start in (0, 128)]
        tables += halves
        digit_rows = []
        for d in range(LOW):
            place = (lanes * LOW + d) & 127
            near, far = (
                jnp.take_along_axis(half, place, axis=1, mode="promise_in_bounds") for half in halves
            )
            digit_rows.append(jnp.where(lanes < 128 // LOW, near, far))
        by_digit.append(jnp.concatenate(digit_rows, axis=0)[:, :HIGH].astype(bf16))
    plan_ref[...] = block_ref[...]
    scale = jnp.broadcast_to(block_ref[groups : groups + 1, :], (GROUP, rows))
    packed = block_ref[:groups, :].astype(jnp.int32)
    for book in range(2):
        code = (packed & 255) if book == 0 else (packed >> 8)
        digit_ref[2 * book] = (code & (LOW - 1)).astype(f32)
        digit_ref[2 * book + 1] = (code >> 3).astype(f32)
    at = lax.broadcasted_iota(jnp.int32, (16, rows), 0)
    high_rows = [(16 * d + at).astype(f32).astype(bf16) for d in range(HIGH // 16)]
    zero, one = jnp.zeros((16, rows), bf16), jnp.ones((16, rows), bf16)

    def picked(book, half, place):
        return jnp.take_along_axis(tables[2 * book + half], place, axis=1, mode="promise_in_bounds")

    def by_gather(g):
        both = jnp.broadcast_to(block_ref[pl.ds(g, 1), :], (GROUP, rows)).astype(jnp.int32)
        parts = []
        for start in range(0, rows, 128):
            packed = both[:, start : start + 128]
            total = None
            for book in range(2):
                code = (packed & 255) if book == 0 else (packed >> 8)
                place = code & 127
                entry = jnp.where(code >= 128, picked(book, 1, place), picked(book, 0, place))
                total = entry if total is None else total + entry
            parts.append(total * scale[:, start : start + 128])
        return jnp.concatenate(parts, axis=1)

    def by_product(g):
        total = None
        for book in range(2):
            high = jnp.broadcast_to(digit_ref[2 * book + 1, pl.ds(g, 1), :], (16, rows)).astype(bf16)
            hot = jnp.concatenate([jnp.where(high == r, one, zero) for r in high_rows], axis=0)
            near = jnp.dot(by_digit[book], hot, preferred_element_type=f32)
            low = jnp.broadcast_to(digit_ref[2 * book, pl.ds(g, 1), :], (GROUP, rows))
            entry = near[:GROUP]
            for d in range(1, LOW):
                entry = jnp.where(low == float(d), near[d * GROUP : (d + 1) * GROUP], entry)
            total = entry if total is None else total + entry
        return total * scale

    chunk = 16

    def step(i, carry):
        for k in range(0, chunk, 2):
            g = i * chunk + k
            pair = jnp.concatenate([by_gather(g), by_product(g + 1)], axis=0)
            weight_ref[pl.ds(pl.multiple_of(g * GROUP, 16), 16), :] = pair.astype(bf16)
        return carry

    lax.fori_loop(0, groups // chunk, step, 0, unroll=2)


def dequantize(block, books, at, blocks, groups, before=()):
    rows = block.shape[1]
    return pl.pallas_call(
        dequant_kernel,
        grid=(1,),
        in_specs=[
            pl.BlockSpec(memory_space=pltpu.VMEM),
            pl.BlockSpec(books[0].shape, lambda i: (0, 0)),
            pl.BlockSpec(books[1].shape, lambda i: (0, 0)),
        ]
        + [pl.BlockSpec(memory_space=pl.ANY)] * len(before),
        out_specs=[
            pl.BlockSpec((None, groups * GROUP, rows), lambda i: (at, 0, 0)),
            pl.BlockSpec((None, *block.shape), lambda i: (at, 0, 0)),
        ],
        out_shape=[
            jax.ShapeDtypeStruct((blocks, groups * GROUP, rows), bf16),
            jax.ShapeDtypeStruct((blocks, *block.shape), f32),
        ],
        scratch_shapes=[pltpu.VMEM((4, groups, rows), f32)],
        input_output_aliases={3: 0, 4: 1} if before else {},
        cost_estimate=pl.CostEstimate(
            flops=8_000_000_000, transcendentals=0, bytes_accessed=1_500_000
        ),
        name="dequant",
    )(block, *books, *before)


def project_kernel(core_ref, att_ref, weight_ref, keep_ref, send_ref, all_ref):
    steps, tokens, width = att_ref.shape
    blocks, _, rows = weight_ref.shape
    half = tokens // 2
    for i in range(blocks):
        total = None
        for z in range(steps):
            tile = weight_ref[i, z * width : (z + 1) * width, :]
            part = jnp.dot(att_ref[z], tile, preferred_element_type=f32)
            total = part if total is None else total + part
        all_ref[...] = total
        columns = slice(i * rows, (i + 1) * rows)
        for out_ref, who in ((keep_ref, core_ref[0]), (send_ref, 1 - core_ref[0])):
            out_ref[:, columns] = all_ref[pl.ds(pl.multiple_of(who * half, half), half), :]


def project(core, attended, weight):
    _, tokens, _ = attended.shape
    blocks, _, rows = weight.shape
    out = jax.ShapeDtypeStruct((tokens // 2, blocks * rows), f32)
    whole = pl.BlockSpec(memory_space=pltpu.VMEM)
    return pl.pallas_call(
        project_kernel,
        in_specs=[pl.BlockSpec(memory_space=pltpu.SMEM), whole, whole],
        out_specs=[whole, whole],
        out_shape=[out, out],
        scratch_shapes=[pltpu.VMEM((tokens, rows), f32)],
        compiler_params=pltpu.CompilerParams(vmem_limit_bytes=14 << 20),
        name="project",
    )(core, attended, weight)


def bins_kernel(scaling, *refs):
    own_att_ref, their_att_ref, own_misfit_ref, their_misfit_ref = refs[:4]
    plan_ref, bins_ref, grad_ref, digit_ref = refs[4:]
    groups, rows = digit_ref.shape[1:]
    steps, _, width = own_att_ref.shape
    scale = plan_ref[groups : groups + 1, :] * scaling
    for z in range(steps):
        weight_grad = None
        for att_ref, misfit_ref in ((own_att_ref, own_misfit_ref), (their_att_ref, their_misfit_ref)):
            part = lax.dot_general(
                att_ref[z], misfit_ref[...], (((0,), (0,)), ((), ())), preferred_element_type=f32
            )
            weight_grad = part if weight_grad is None else weight_grad + part
        grad_ref[z * width : (z + 1) * width, :] = weight_grad * scale
    packed = plan_ref[:groups, :].astype(jnp.int32)
    for book in range(2):
        code = (packed & 255) if book == 0 else (packed >> 8)
        digit_ref[2 * book] = (code & (LOW - 1)).astype(f32)
        digit_ref[2 * book + 1] = (code >> 3).astype(f32)
    at = lax.broadcasted_iota(jnp.int32, (16, rows), 0)
    low_rows = [(2 * d + (at >= 8).astype(jnp.int32)).astype(f32).astype(bf16) for d in range(LOW // 2)]
    high_rows = [(16 * d + at).astype(f32).astype(bf16) for d in range(HIGH // 16)]
    zero, one = jnp.zeros((16, rows), bf16), jnp.ones((16, rows), bf16)
    chunk = 8

    def digit(which, g):
        return jnp.broadcast_to(digit_ref[which, pl.ds(g, 1), :], (16, rows)).astype(bf16)

    def step(i, totals):
        twice = []
        for k in range(chunk):
            entry = grad_ref[pl.ds(pl.multiple_of((i * chunk + k) * GROUP, GROUP), GROUP), :]
            twice.append(jnp.concatenate([entry, entry], axis=0).astype(bf16))
        done = []
        for book in range(2):
            highs, lows = [], []
            for k in range(chunk):
                low, high = digit(2 * book, i * chunk + k), digit(2 * book + 1, i * chunk + k)
                lows.append(
                    jnp.concatenate([jnp.where(low == r, twice[k], zero) for r in low_rows], axis=0)
                )
                highs.append(
                    jnp.concatenate([jnp.where(high == r, one, zero) for r in high_rows], axis=0)
                )
            part = lax.dot_general(
                jnp.concatenate(highs, axis=1),
                jnp.concatenate(lows, axis=1),
                (((1,), (1,)), ((), ())),
                preferred_element_type=f32,
            )
            done.append(totals[book] + part)
        return tuple(done)

    empty = jnp.zeros((HIGH, LOW * GROUP), f32)
    totals = lax.fori_loop(0, groups // chunk, step, (empty, empty), unroll=2)

    @pl.when(pl.program_id(0) == 0)
    def _():
        bins_ref[...] = jnp.zeros_like(bins_ref)

    for book in range(2):
        bins_ref[book] += totals[book]


def bin_gradients(own, theirs, plan, groups, scaling):
    steps, tokens, width = own[0].shape
    blocks, depth, rows = plan.shape
    whole = pl.BlockSpec(memory_space=pltpu.VMEM)
    return pl.pallas_call(
        lambda *refs: bins_kernel(scaling, *refs),
        grid=(blocks // 2,),
        in_specs=[
            whole,
            whole,
            pl.BlockSpec((tokens, rows), lambda i: (0, 2 * i)),
            pl.BlockSpec((tokens, rows), lambda i: (0, i)),
            pl.BlockSpec((None, depth, rows), lambda i: (2 * i, 0, 0)),
        ],
        out_specs=pl.BlockSpec((2, HIGH, LOW * GROUP), lambda i: (0, 0, 0)),
        out_shape=jax.ShapeDtypeStruct((2, HIGH, LOW * GROUP), f32),
        scratch_shapes=[
            pltpu.VMEM((steps * width, rows), f32),
            pltpu.VMEM((4, groups, rows), f32),
        ],
        cost_estimate=pl.CostEstimate(
            flops=blocks * 4_000_000_000, transcendentals=0, bytes_accessed=blocks * 1_000_000
        ),
        compiler_params=pltpu.CompilerParams(vmem_limit_bytes=16 << 20),
        name="bins",
    )(own[0], theirs[0], own[1], theirs[1], plan)


def attend(queries, keys, values, query_places, key_places):
    scores = jnp.einsum("qd,kd->qk", queries, keys, preferred_element_type=f32) / math.sqrt(HEAD_DIM)
    allowed = key_places[None, :] <= query_places[:, None]
    row_max = jnp.max(jnp.where(allowed, scores, -1e30), axis=-1, keepdims=True)
    exponent = jnp.where(allowed, jnp.exp(scores - row_max), 0.0)
    row_sum = jnp.sum(exponent, axis=-1, keepdims=True)
    weighted = jnp.einsum("qk,kd->qd", exponent.astype(bf16), values, preferred_element_type=f32)
    return (weighted / row_sum).astype(bf16)


def device_part(
    queries, key_rows, values, code_first, code_second, book_first, book_second, scales, target
):
    tok_rows, _ = queries.shape
    high, across = lax.axis_index("tok_0"), lax.axis_index("tok_1")
    count_across = lax.axis_size("tok_1")
    lane, core = lax.axis_index("col_0"), lax.axis_index("col_1")
    count_lane, count_col = lax.axis_size("col_0"), lax.axis_size(COL)
    rows = code_first.shape[0]
    tokens = lax.axis_size(TOK) * tok_rows

    def of_head(head):
        picked = [
            lax.dynamic_slice_in_dim(array, head * HEAD_DIM, HEAD_DIM, 1)
            for array in (queries, key_rows, values)
        ]
        return jnp.concatenate(picked, axis=1)

    mine = of_head(high)
    both = jnp.concatenate(in_order(mine, swap(of_head(1 - high), "tok_0"), high))
    pairs = copies(both[:, HEAD_DIM:], "tok_1")
    block = lax.iota(jnp.int32, 2)[:, None] * (count_across * tok_rows)
    block = block + lax.iota(jnp.int32, tok_rows)[None, :]
    query_places = (block + across * tok_rows).reshape(-1)
    key_places = lax.iota(jnp.int32, count_across)[:, None, None] * tok_rows + block[None]
    pairs = pairs.reshape(tokens, 2 * HEAD_DIM)
    head_out = attend(
        both[:, :HEAD_DIM], pairs[:, :HEAD_DIM], pairs[:, HEAD_DIM:], query_places, key_places.reshape(-1)
    )
    other_out = swap(head_out, "tok_0")
    attended = copies(jnp.concatenate(in_order(head_out, other_out, high), axis=1), "row")

    own_codes = (code_first + ENTRIES * code_second).T.astype(f32)
    groups = own_codes.shape[0]
    share = tok_rows // count_lane
    wanted = target.reshape(2, count_across, count_lane, share, rows)
    wanted = lax.dynamic_index_in_dim(wanted, core, 0, keepdims=False)
    wanted = lax.dynamic_index_in_dim(wanted, lane, 1, keepdims=False).astype(f32)
    own_scales = jnp.broadcast_to(scales[None], (8, rows))

    def block_for(peer):
        part = lax.dynamic_index_in_dim(wanted, peer, 0, keepdims=False)
        return jnp.concatenate([own_codes, own_scales, part], axis=0)

    own_block = block_for(across)
    books = (book_first.T, book_second.T)
    received = [own_block]
    built = dequantize(own_block, books, 0, count_across, groups)
    for k in range(1, count_across):
        sent, _ = lax.optimization_barrier((block_for((across + count_across - k) % count_across), pairs))
        route = [((i + k) % count_across, i) for i in range(count_across)]
        received.append(lax.ppermute(sent, "tok_1", route))
        built = dequantize(received[k], books, k, count_across, groups, built)
    weight, plan = built

    keep, send = project(core[None], attended, weight)
    pair = [(0, 1), (1, 0), (2, 3), (3, 2)]
    their_attended = lax.ppermute(attended, "tok_1", pair)
    half_sum = (keep + swap(send, "col_1")).astype(bf16)
    parts = exchange(half_sum.reshape(count_lane, share, -1), "col_0")
    output = jnp.sum(parts.astype(f32), axis=0)
    misfit_share = (output - plan[:, groups + 8 :].transpose(1, 0, 2).reshape(share, -1)).astype(bf16)
    misfit_half = copies(misfit_share, "col_0").reshape(tok_rows, -1)
    even = across % 2 == 0

    def pairs_blocks(array):
        second, fourth = array[:, rows : 2 * rows], array[:, 3 * rows :]
        return jnp.where(even, second, fourth), jnp.where(even, fourth, second)

    other_half = swap(misfit_half, "col_1")
    their_half = lax.ppermute(jnp.concatenate(pairs_blocks(misfit_half), axis=1), "tok_1", pair)
    misfit = jnp.concatenate(in_order(misfit_half, other_half, core), axis=0)
    their_other = swap(their_half, "col_1")
    their_misfit = jnp.concatenate(in_order(their_half, their_other, core), axis=0)
    blocks = [misfit[:, k * rows : (k + 1) * rows] for k in range(count_across)]
    pairs_next = pairs_blocks(misfit)[1]
    from_across = lax.ppermute(blocks[2], "tok_1", [(0, 2), (1, 3), (2, 0), (3, 1)])
    from_beside = lax.ppermute(pairs_next, "tok_1", [(1, 2), (2, 1), (3, 0), (0, 3)])
    step = jnp.where(even, 1, count_across - 1)
    out_pieces = (
        (blocks[0], across),
        (their_misfit[:, :rows], (across + step) % count_across),
        (from_across, (across + 2) % count_across),
        (from_beside, (across + count_across - step) % count_across),
    )

    scale_part = jnp.sum(misfit_share.astype(f32) * output, axis=0).reshape(count_across, -1, 128)
    extra = scale_part.shape[1]
    scale_part = jnp.concatenate([scale_part, scale_part], axis=0)
    start = (count_across - across) % count_across
    scale_part = in_two(lax.dynamic_slice_in_dim(scale_part, start, count_across, 0), 1)
    theirs = (their_attended, their_misfit)
    bins = bin_gradients((attended, misfit), theirs, plan, groups, 1.0 / tokens)

    count_row = lax.axis_size("row")
    bins = bins.reshape(-1, 128).astype(bf16)
    bins = jnp.broadcast_to(bins[None, None], (count_row, count_across, *bins.shape))
    scale_part = jnp.broadcast_to(scale_part[None], (count_row, *scale_part.shape))
    sums = jnp.concatenate([bins, scale_part], axis=2).reshape(count_row * count_across, -1, 128)
    sums = exchange(sums, ("row", "tok_1"))
    own_row = sums.reshape(count_row, count_across, -1, 128)[:, :, -2 * extra :]
    own_row = lax.dynamic_index_in_dim(own_row, lax.axis_index("row"), 0, keepdims=False)
    own_row = jnp.sum(own_row.astype(f32), axis=0)
    scale_part = in_two(own_row[:extra] + own_row[extra:], 0)
    bins = jnp.sum(sums[:, : -2 * extra].astype(f32), axis=0).astype(bf16)
    sums = copies(jnp.concatenate([bins, scale_part]), COL + ("tok_0",))
    scale_part = sums.reshape(count_col, 2, -1, 128)[:, :, -2 * extra :]
    scale_part = lax.dynamic_index_in_dim(scale_part, high, 1, keepdims=False)
    scale_part = jnp.sum(scale_part.astype(f32), axis=0)
    grad_scales = (scale_part[:extra] + scale_part[extra:]).reshape(rows) / (scales * tokens)
    grad_books = jnp.sum(sums[:, : -2 * extra].astype(f32), axis=0).reshape(2, ENTRIES, GROUP)

    misfit_out = jnp.zeros((2, count_across, tok_rows, rows), bf16)
    for piece, peer in out_pieces:
        piece = piece.reshape(2, 1, tok_rows, rows)
        misfit_out = lax.dynamic_update_slice_in_dim(misfit_out, piece, peer, 1)
    return misfit_out.reshape(tokens, rows), grad_scales, grad_books


def solution(mesh):
    split = Mesh(
        mesh.devices.reshape(4, 2, mesh.shape["row"], 2, 4),
        ("col_0", "col_1", "row", "tok_0", "tok_1"),
    )
    return jax.shard_map(
        device_part,
        mesh=split,
        in_specs=(
            P(TOK, COL_ROW),
            P(TOK, COL_ROW),
            P(TOK, COL_ROW),
            P(ROW_TOK, COL),
            P(ROW_TOK, COL),
            P(),
            P(),
            P(ROW_TOK),
            P(None, ROW_TOK),
        ),
        out_specs=(P(None, ROW_TOK), P(ROW_TOK), P()),
        check_vma=False,
    )
```

```python
import math

import jax
import jax.numpy as jnp
from jax import lax
from jax.experimental import pallas as pl
from jax.experimental.pallas import tpu as pltpu
from jax.sharding import Mesh
from jax.sharding import PartitionSpec as P


HEAD_DIM = 128
ENTRIES = 256
GROUP = 8
LOW = 8
HIGH = ENTRIES // LOW
TOK = ("tok_0", "tok_1")
ROW_TOK = ("row", "tok_0", "tok_1")
COL = ("col_0", "col_1")
COL_ROW = ("col_0", "col_1", "row")
f32, bf16 = jnp.float32, jnp.bfloat16


def exchange(pieces, axis):
    return lax.all_to_all(pieces, axis, 0, 0, tiled=True)


def copies(array, axis):
    pieces = jnp.broadcast_to(array[None], (lax.axis_size(axis), *array.shape))
    return exchange(pieces, axis)


def in_two(array, axis):
    upper = array.astype(bf16)
    return jnp.concatenate([upper, (array - upper.astype(f32)).astype(bf16)], axis=axis)


def swap(array, axis):
    return lax.ppermute(array, axis, [(0, 1), (1, 0)])


def in_order(mine, theirs, place):
    first = place == 0
    return jnp.where(first, mine, theirs), jnp.where(first, theirs, mine)


def dequant_kernel(block_ref, first_ref, second_ref, *refs):
    weight_ref, plan_ref, digit_ref = refs[-3:]
    groups, rows = weight_ref.shape[0] // GROUP, weight_ref.shape[1]
    tables, by_digit = [], []
    lanes = lax.broadcasted_iota(jnp.int32, (GROUP, 128), 1)
    for book_ref in (first_ref, second_ref):
        halves = [book_ref[:, start : start + 128].astype(f32) for start in (0, 128)]
        tables += halves
        digit_rows = []
        for d in range(LOW):
            place = (lanes * LOW + d) & 127
            near, far = (
                jnp.take_along_axis(half, place, axis=1, mode="promise_in_bounds") for half in halves
            )
            digit_rows.append(jnp.where(lanes < 128 // LOW, near, far))
        by_digit.append(jnp.concatenate(digit_rows, axis=0)[:, :HIGH].astype(bf16))
    plan_ref[...] = block_ref[...]
    scale = jnp.broadcast_to(block_ref[groups : groups + 1, :], (GROUP, rows))
    packed = block_ref[:groups, :].astype(jnp.int32)
    for book in range(2):
        code = (packed & 255) if book == 0 else (packed >> 8)
        digit_ref[2 * book] = (code & (LOW - 1)).astype(f32)
        digit_ref[2 * book + 1] = (code >> 3).astype(f32)
    at = lax.broadcasted_iota(jnp.int32, (16, rows), 0)
    high_rows = [(16 * d + at).astype(f32).astype(bf16) for d in range(HIGH // 16)]
    zero, one = jnp.zeros((16, rows), bf16), jnp.ones((16, rows), bf16)

    def picked(book, half, place):
        return jnp.take_along_axis(tables[2 * book + half], place, axis=1, mode="promise_in_bounds")

    def by_gather(g):
        both = jnp.broadcast_to(block_ref[pl.ds(g, 1), :], (GROUP, rows)).astype(jnp.int32)
        parts = []
        for start in range(0, rows, 128):
            packed = both[:, start : start + 128]
            total = None
            for book in range(2):
                code = (packed & 255) if book == 0 else (packed >> 8)
                place = code & 127
                entry = jnp.where(code >= 128, picked(book, 1, place), picked(book, 0, place))
                total = entry if total is None else total + entry
            parts.append(total * scale[:, start : start + 128])
        return jnp.concatenate(parts, axis=1)

    def by_product(g):
        total = None
        for book in range(2):
            high = jnp.broadcast_to(digit_ref[2 * book + 1, pl.ds(g, 1), :], (16, rows)).astype(bf16)
            hot = jnp.concatenate([jnp.where(high == r, one, zero) for r in high_rows], axis=0)
            near = jnp.dot(by_digit[book], hot, preferred_element_type=f32)
            low = jnp.broadcast_to(digit_ref[2 * book, pl.ds(g, 1), :], (GROUP, rows))
            entry = near[:GROUP]
            for d in range(1, LOW):
                entry = jnp.where(low == float(d), near[d * GROUP : (d + 1) * GROUP], entry)
            total = entry if total is None else total + entry
        return total * scale

    chunk = 16

    def step(i, carry):
        for k in range(0, chunk, 2):
            g = i * chunk + k
            pair = jnp.concatenate([by_gather(g), by_product(g + 1)], axis=0)
            weight_ref[pl.ds(pl.multiple_of(g * GROUP, 16), 16), :] = pair.astype(bf16)
        return carry

    lax.fori_loop(0, groups // chunk, step, 0, unroll=2)


def dequantize(block, books, at, blocks, groups, before=()):
    rows = block.shape[1]
    return pl.pallas_call(
        dequant_kernel,
        grid=(1,),
        in_specs=[
            pl.BlockSpec(memory_space=pltpu.VMEM),
            pl.BlockSpec(books[0].shape, lambda i: (0, 0)),
            pl.BlockSpec(books[1].shape, lambda i: (0, 0)),
        ]
        + [pl.BlockSpec(memory_space=pl.ANY)] * len(before),
        out_specs=[
            pl.BlockSpec((None, groups * GROUP, rows), lambda i: (at, 0, 0)),
            pl.BlockSpec((None, *block.shape), lambda i: (at, 0, 0)),
        ],
        out_shape=[
            jax.ShapeDtypeStruct((blocks, groups * GROUP, rows), bf16),
            jax.ShapeDtypeStruct((blocks, *block.shape), f32),
        ],
        scratch_shapes=[pltpu.VMEM((4, groups, rows), f32)],
        input_output_aliases={3: 0, 4: 1} if before else {},
        cost_estimate=pl.CostEstimate(
            flops=8_000_000_000, transcendentals=0, bytes_accessed=1_500_000
        ),
        name="dequant",
    )(block, *books, *before)


def project_kernel(core_ref, att_ref, weight_ref, keep_ref, send_ref, all_ref):
    steps, tokens, width = att_ref.shape
    blocks, _, rows = weight_ref.shape
    half = tokens // 2
    for i in range(blocks):
        total = None
        for z in range(steps):
            tile = weight_ref[i, z * width : (z + 1) * width, :]
            part = jnp.dot(att_ref[z], tile, preferred_element_type=f32)
            total = part if total is None else total + part
        all_ref[...] = total
        columns = slice(i * rows, (i + 1) * rows)
        for out_ref, who in ((keep_ref, core_ref[0]), (send_ref, 1 - core_ref[0])):
            out_ref[:, columns] = all_ref[pl.ds(pl.multiple_of(who * half, half), half), :]


def project(core, attended, weight):
    _, tokens, _ = attended.shape
    blocks, _, rows = weight.shape
    out = jax.ShapeDtypeStruct((tokens // 2, blocks * rows), f32)
    whole = pl.BlockSpec(memory_space=pltpu.VMEM)
    return pl.pallas_call(
        project_kernel,
        in_specs=[pl.BlockSpec(memory_space=pltpu.SMEM), whole, whole],
        out_specs=[whole, whole],
        out_shape=[out, out],
        scratch_shapes=[pltpu.VMEM((tokens, rows), f32)],
        compiler_params=pltpu.CompilerParams(vmem_limit_bytes=14 << 20),
        name="project",
    )(core, attended, weight)


def bins_kernel(scaling, *refs):
    own_att_ref, their_att_ref, own_misfit_ref, their_misfit_ref = refs[:4]
    plan_ref, bins_ref, grad_ref, digit_ref = refs[4:]
    groups, rows = digit_ref.shape[1:]
    steps, _, width = own_att_ref.shape
    scale = plan_ref[groups : groups + 1, :] * scaling
    for z in range(steps):
        weight_grad = None
        for att_ref, misfit_ref in ((own_att_ref, own_misfit_ref), (their_att_ref, their_misfit_ref)):
            part = lax.dot_general(
                att_ref[z], misfit_ref[...], (((0,), (0,)), ((), ())), preferred_element_type=f32
            )
            weight_grad = part if weight_grad is None else weight_grad + part
        grad_ref[z * width : (z + 1) * width, :] = weight_grad * scale
    packed = plan_ref[:groups, :].astype(jnp.int32)
    for book in range(2):
        code = (packed & 255) if book == 0 else (packed >> 8)
        digit_ref[2 * book] = (code & (LOW - 1)).astype(f32)
        digit_ref[2 * book + 1] = (code >> 3).astype(f32)
    at = lax.broadcasted_iota(jnp.int32, (16, rows), 0)
    low_rows = [(2 * d + (at >= 8).astype(jnp.int32)).astype(f32).astype(bf16) for d in range(LOW // 2)]
    high_rows = [(16 * d + at).astype(f32).astype(bf16) for d in range(HIGH // 16)]
    zero, one = jnp.zeros((16, rows), bf16), jnp.ones((16, rows), bf16)
    chunk = 8

    def digit(which, g):
        return jnp.broadcast_to(digit_ref[which, pl.ds(g, 1), :], (16, rows)).astype(bf16)

    def step(i, totals):
        twice = []
        for k in range(chunk):
            entry = grad_ref[pl.ds(pl.multiple_of((i * chunk + k) * GROUP, GROUP), GROUP), :]
            twice.append(jnp.concatenate([entry, entry], axis=0).astype(bf16))
        done = []
        for book in range(2):
            highs, lows = [], []
            for k in range(chunk):
                low, high = digit(2 * book, i * chunk + k), digit(2 * book + 1, i * chunk + k)
                lows.append(
                    jnp.concatenate([jnp.where(low == r, twice[k], zero) for r in low_rows], axis=0)
                )
                highs.append(
                    jnp.concatenate([jnp.where(high == r, one, zero) for r in high_rows], axis=0)
                )
            part = lax.dot_general(
                jnp.concatenate(highs, axis=1),
                jnp.concatenate(lows, axis=1),
                (((1,), (1,)), ((), ())),
                preferred_element_type=f32,
            )
            done.append(totals[book] + part)
        return tuple(done)

    empty = jnp.zeros((HIGH, LOW * GROUP), f32)
    totals = lax.fori_loop(0, groups // chunk, step, (empty, empty), unroll=2)

    @pl.when(pl.program_id(0) == 0)
    def _():
        bins_ref[...] = jnp.zeros_like(bins_ref)

    for book in range(2):
        bins_ref[book] += totals[book]


def bin_gradients(own, theirs, plan, groups, scaling):
    steps, tokens, width = own[0].shape
    blocks, depth, rows = plan.shape
    whole = pl.BlockSpec(memory_space=pltpu.VMEM)
    return pl.pallas_call(
        lambda *refs: bins_kernel(scaling, *refs),
        grid=(blocks // 2,),
        in_specs=[
            whole,
            whole,
            pl.BlockSpec((tokens, rows), lambda i: (0, 2 * i)),
            pl.BlockSpec((tokens, rows), lambda i: (0, i)),
            pl.BlockSpec((None, depth, rows), lambda i: (2 * i, 0, 0)),
        ],
        out_specs=pl.BlockSpec((2, HIGH, LOW * GROUP), lambda i: (0, 0, 0)),
        out_shape=jax.ShapeDtypeStruct((2, HIGH, LOW * GROUP), f32),
        scratch_shapes=[
            pltpu.VMEM((steps * width, rows), f32),
            pltpu.VMEM((4, groups, rows), f32),
        ],
        cost_estimate=pl.CostEstimate(
            flops=blocks * 4_000_000_000, transcendentals=0, bytes_accessed=blocks * 1_000_000
        ),
        compiler_params=pltpu.CompilerParams(vmem_limit_bytes=16 << 20),
        name="bins",
    )(own[0], theirs[0], own[1], theirs[1], plan)


def attend(queries, keys, values, query_places, key_places):
    scores = jnp.einsum("qd,kd->qk", queries, keys, preferred_element_type=f32) / math.sqrt(HEAD_DIM)
    allowed = key_places[None, :] <= query_places[:, None]
    row_max = jnp.max(jnp.where(allowed, scores, -1e30), axis=-1, keepdims=True)
    exponent = jnp.where(allowed, jnp.exp(scores - row_max), 0.0)
    row_sum = jnp.sum(exponent, axis=-1, keepdims=True)
    weighted = jnp.einsum("qk,kd->qd", exponent.astype(bf16), values, preferred_element_type=f32)
    return (weighted / row_sum).astype(bf16)


def device_part(
    queries, key_rows, values, code_first, code_second, book_first, book_second, scales, target
):
    tok_rows, _ = queries.shape
    high, across = lax.axis_index("tok_0"), lax.axis_index("tok_1")
    count_across = lax.axis_size("tok_1")
    lane, core = lax.axis_index("col_0"), lax.axis_index("col_1")
    count_lane, count_col = lax.axis_size("col_0"), lax.axis_size(COL)
    rows = code_first.shape[0]
    tokens = lax.axis_size(TOK) * tok_rows

    def of_head(head):
        picked = [
            lax.dynamic_slice_in_dim(array, head * HEAD_DIM, HEAD_DIM, 1)
            for array in (queries, key_rows, values)
        ]
        return jnp.concatenate(picked, axis=1)

    mine = of_head(high)
    both = jnp.concatenate(in_order(mine, swap(of_head(1 - high), "tok_0"), high))
    pairs = copies(both[:, HEAD_DIM:], "tok_1")
    block = lax.iota(jnp.int32, 2)[:, None] * (count_across * tok_rows)
    block = block + lax.iota(jnp.int32, tok_rows)[None, :]
    query_places = (block + across * tok_rows).reshape(-1)
    key_places = lax.iota(jnp.int32, count_across)[:, None, None] * tok_rows + block[None]
    pairs = pairs.reshape(tokens, 2 * HEAD_DIM)
    head_out = attend(
        both[:, :HEAD_DIM], pairs[:, :HEAD_DIM], pairs[:, HEAD_DIM:], query_places, key_places.reshape(-1)
    )
    other_out = swap(head_out, "tok_0")
    attended = copies(jnp.concatenate(in_order(head_out, other_out, high), axis=1), "row")

    own_codes = (code_first + ENTRIES * code_second).T.astype(f32)
    groups = own_codes.shape[0]
    share = tok_rows // count_lane
    wanted = target.reshape(2, count_across, count_lane, share, rows)
    wanted = lax.dynamic_index_in_dim(wanted, core, 0, keepdims=False)
    wanted = lax.dynamic_index_in_dim(wanted, lane, 1, keepdims=False).astype(f32)
    own_scales = jnp.broadcast_to(scales[None], (8, rows))

    def block_for(peer):
        part = lax.dynamic_index_in_dim(wanted, peer, 0, keepdims=False)
        return jnp.concatenate([own_codes, own_scales, part], axis=0)

    own_block = block_for(across)
    books = (book_first.T, book_second.T)
    received = [own_block]
    built = dequantize(own_block, books, 0, count_across, groups)
    for k in range(1, count_across):
        sent, _ = lax.optimization_barrier((block_for((across + count_across - k) % count_across), pairs))
        route = [((i + k) % count_across, i) for i in range(count_across)]
        received.append(lax.ppermute(sent, "tok_1", route))
        built = dequantize(received[k], books, k, count_across, groups, built)
    weight, plan = built

    keep, send = project(core[None], attended, weight)
    pair = [(0, 1), (1, 0), (2, 3), (3, 2)]
    their_attended = lax.ppermute(attended, "tok_1", pair)
    half_sum = (keep + swap(send, "col_1")).astype(bf16)
    parts = exchange(half_sum.reshape(count_lane, share, -1), "col_0")
    output = jnp.sum(parts.astype(f32), axis=0)
    misfit_share = (output - plan[:, groups + 8 :].transpose(1, 0, 2).reshape(share, -1)).astype(bf16)
    misfit_half = copies(misfit_share, "col_0").reshape(tok_rows, -1)
    other_half = swap(misfit_half, "col_1")
    misfit = jnp.concatenate(in_order(misfit_half, other_half, core), axis=0)

    even = across % 2 == 0
    blocks = [misfit[:, k * rows : (k + 1) * rows] for k in range(count_across)]
    pairs_own, pairs_next = jnp.where(even, blocks[1], blocks[3]), jnp.where(even, blocks[3], blocks[1])
    their_misfit = lax.ppermute(jnp.concatenate([pairs_own, pairs_next], axis=1), "tok_1", pair)
    from_across = lax.ppermute(blocks[2], "tok_1", [(0, 2), (1, 3), (2, 0), (3, 1)])
    from_beside = lax.ppermute(pairs_next, "tok_1", [(1, 2), (2, 1), (3, 0), (0, 3)])
    step = jnp.where(even, 1, count_across - 1)
    out_pieces = (
        (blocks[0], across),
        (their_misfit[:, :rows], (across + step) % count_across),
        (from_across, (across + 2) % count_across),
        (from_beside, (across + count_across - step) % count_across),
    )

    scale_part = jnp.sum(misfit_share.astype(f32) * output, axis=0).reshape(count_across, -1, 128)
    extra = scale_part.shape[1]
    scale_part = jnp.concatenate([scale_part, scale_part], axis=0)
    start = (count_across - across) % count_across
    scale_part = in_two(lax.dynamic_slice_in_dim(scale_part, start, count_across, 0), 1)
    theirs = (their_attended, their_misfit)
    bins = bin_gradients((attended, misfit), theirs, plan, groups, 1.0 / tokens)

    count_row = lax.axis_size("row")
    bins = bins.reshape(-1, 128).astype(bf16)
    bins = jnp.broadcast_to(bins[None, None], (count_row, count_across, *bins.shape))
    scale_part = jnp.broadcast_to(scale_part[None], (count_row, *scale_part.shape))
    sums = jnp.concatenate([bins, scale_part], axis=2).reshape(count_row * count_across, -1, 128)
    sums = exchange(sums, ("row", "tok_1"))
    own_row = sums.reshape(count_row, count_across, -1, 128)[:, :, -2 * extra :]
    own_row = lax.dynamic_index_in_dim(own_row, lax.axis_index("row"), 0, keepdims=False)
    own_row = jnp.sum(own_row.astype(f32), axis=0)
    scale_part = in_two(own_row[:extra] + own_row[extra:], 0)
    bins = jnp.sum(sums[:, : -2 * extra].astype(f32), axis=0).astype(bf16)
    sums = copies(jnp.concatenate([bins, scale_part]), COL + ("tok_0",))
    scale_part = sums.reshape(count_col, 2, -1, 128)[:, :, -2 * extra :]
    scale_part = lax.dynamic_index_in_dim(scale_part, high, 1, keepdims=False)
    scale_part = jnp.sum(scale_part.astype(f32), axis=0)
    grad_scales = (scale_part[:extra] + scale_part[extra:]).reshape(rows) / (scales * tokens)
    grad_books = jnp.sum(sums[:, : -2 * extra].astype(f32), axis=0).reshape(2, ENTRIES, GROUP)

    misfit_out = jnp.zeros((2, count_across, tok_rows, rows), bf16)
    for piece, peer in out_pieces:
        piece = piece.reshape(2, 1, tok_rows, rows)
        misfit_out = lax.dynamic_update_slice_in_dim(misfit_out, piece, peer, 1)
    return misfit_out.reshape(tokens, rows), grad_scales, grad_books


def solution(mesh):
    split = Mesh(
        mesh.devices.reshape(4, 2, mesh.shape["row"], 2, 4),
        ("col_0", "col_1", "row", "tok_0", "tok_1"),
    )
    return jax.shard_map(
        device_part,
        mesh=split,
        in_specs=(
            P(TOK, COL_ROW),
            P(TOK, COL_ROW),
            P(TOK, COL_ROW),
            P(ROW_TOK, COL),
            P(ROW_TOK, COL),
            P(),
            P(),
            P(ROW_TOK),
            P(None, ROW_TOK),
        ),
        out_specs=(P(None, ROW_TOK), P(ROW_TOK), P()),
        check_vma=False,
    )
```
